32 devices in a mesh: tm: 8 (over y, x, core), tile: 4 (over z).
Axes of the slice: x: 2, y: 2, z: 4, core: 2. Of those that a mesh axis runs over, the one named last changes fastest.
Arguments:
- local_inv: bfloat16 [16, 2048, 2048], P('tm', None, 'tile'), as said below
- seed_inv: float32 [8, 2048, 2048], P('tm', None, 'tile'), as said below
- band: float32 [16, 16, 3, 128, 128], P('tm', 'tile'), may hold values from -0.25 to 0.25
- pattern: int32 [16, 16, 3], P('tm', 'tile'), may hold values from 0 to 1, as said below
Outputs:
- sigma_first: float32 [8, 2048, 2048], P('tm', None, 'tile')
- variances: float32 [16, 2048], P('tm', 'tile')
The draws below stay inside these ranges and needn't reach their ends.
Inputs may be any that keep to these rules, and one draw needn't show every extreme that they name: Every entry is 0 or 1; the middle entry pattern[j, b, 1] is 1; pattern[j, 0, 0] and pattern[j, 15, 2] are 0. `local_inv`: each matrix is symmetric. `seed_inv`: each matrix is symmetric.
All inputs are finite; a program needn't handle non-finite values.
Results may differ from the reference program's by a relative error of at most 0.0003.
Values sent between devices are 32-bit elements; how exact they have to be, the bound alone decides.
A program may use at most 128 MiB of HBM per device.

```python
import jax
import jax.numpy as jnp
from jax import lax

TILE_ROWS = 128
BLOCK = 2048
TILES = 16
TBLOCKS = 16
N_TM = 8


def symmetric_field(key, count):
    first = jax.random.fold_in(key, 0)
    third = jax.random.fold_in(key, 2)
    noise = jax.random.normal(first, (count, BLOCK, BLOCK), jnp.float32)
    field = 0.35 * (noise + jnp.swapaxes(noise, 1, 2))
    lift = 1.5 + jax.random.uniform(third, (count, BLOCK), jnp.float32)
    return field + jnp.eye(BLOCK, dtype=jnp.float32)[None] * lift[:, :, None]


def draw_local_inv(key, part):
    return symmetric_field(jax.random.fold_in(key, 11), TBLOCKS).astype(jnp.bfloat16)


def draw_seed_inv(key, part):
    return symmetric_field(jax.random.fold_in(key, 23), N_TM)


def draw_pattern(key, part):
    coins = jax.random.randint(jax.random.fold_in(key, 37), (TBLOCKS, TILES, 3), 0, 4)
    filled = jnp.where(coins > 0, 1, 0)
    column = jnp.arange(3)[None, None, :]
    tile_index = jnp.arange(TILES)[None, :, None]
    filled = jnp.where(column == 1, 1, filled)
    filled = jnp.where((tile_index == 0) & (column == 0), 0, filled)
    filled = jnp.where((tile_index == TILES - 1) & (column == 2), 0, filled)
    return filled.astype(jnp.int32)


def shard_levels(key, dims, pieces, low, largest):
    factor_of = 1.0
    for dim, parts in pieces:
        steps = jax.random.uniform(jax.random.fold_in(jax.random.fold_in(key, 6), dim), (parts,), jnp.float32, low / len(pieces), largest / len(pieces))
        factor_of = factor_of * jnp.repeat(jnp.exp(steps), dims[dim] // parts).reshape((-1,) + (1,) * (len(dims) - 1 - dim))
    return factor_of


def gaussian(stream_key, dims, deviation, reach, cuts=(), held_as=jnp.bfloat16):
    values = deviation * jax.random.normal(stream_key, dims, jnp.float32)
    if cuts:
        values = values * shard_levels(stream_key, dims, cuts, -0.22, 0.18)
    return jnp.clip(values, -reach, reach).astype(held_as)


def setup_inputs(seed: int = 0) -> dict:
    key_of = jax.random.split(jax.random.key(seed), 5)
    return {
        "local_inv": draw_local_inv(jax.random.fold_in(key_of[4], 71), 0),
        "seed_inv": draw_seed_inv(jax.random.fold_in(key_of[4], 71), 0),
        "band": gaussian(key_of[2], (TBLOCKS, TILES, 3, TILE_ROWS, TILE_ROWS), (4 * TILE_ROWS) ** -0.5, 0.25, ((0, 8), (1, 4)), jnp.float32),
        "pattern": draw_pattern(jax.random.fold_in(key_of[4], 71), 0),
    }


HIGH = lax.Precision.HIGHEST


def right_apply(field, weff):
    tiles = weff.shape[0]
    tile_rows = weff.shape[2]
    count = field.shape[0]
    spread = field.reshape(count, tiles, tile_rows)
    padded = jnp.pad(spread, ((0, 0), (1, 1), (0, 0)))
    windows = jnp.stack([padded[:, offset:offset + tiles] for offset in range(3)], axis=2)
    product = jnp.einsum('rbkc,bkcd->rbd', windows, weff, precision=HIGH)
    return product.reshape(count, count)


def left_apply(product, weff):
    tiles = weff.shape[0]
    tile_rows = weff.shape[2]
    count = product.shape[1]
    spread = product.reshape(tiles, tile_rows, count)
    padded = jnp.pad(spread, ((1, 1), (0, 0), (0, 0)))
    windows = jnp.stack([padded[offset:offset + tiles] for offset in range(3)], axis=1)
    result = jnp.einsum('skcd,skce->sde', weff, windows, precision=HIGH)
    return result.reshape(tiles * tile_rows, count)


def reference(local_inv, seed_inv, band, pattern):
    weff = band * pattern.astype(jnp.float32)[..., None, None]
    count = local_inv.shape[1]
    nexts = jnp.concatenate([seed_inv[1:], jnp.zeros_like(seed_inv[:1])], axis=0)
    pairs = local_inv.reshape(N_TM, 2, count, count)
    wpairs = weff.reshape((N_TM, 2) + weff.shape[1:])

    def one_part(items):
        local_pair, w_pair, next_field = items
        sigma_odd = local_pair[1].astype(jnp.float32) + left_apply(right_apply(next_field, w_pair[1]), w_pair[1])
        sigma_even = local_pair[0].astype(jnp.float32) + left_apply(right_apply(sigma_odd, w_pair[0]), w_pair[0])
        return sigma_even, jnp.stack([jnp.diagonal(sigma_even), jnp.diagonal(sigma_odd)])

    sigma_first, diagonals = lax.map(one_part, (pairs, wpairs, nexts))
    variances = diagonals.reshape(2 * N_TM, count)
    return sigma_first, variances
```

```python
import functools

import jax
import jax.numpy as jnp
from jax import lax
from jax.experimental import pallas as pl
from jax.experimental.pallas import tpu as pltpu
from jax.sharding import PartitionSpec as P

F32 = jnp.float32
BF16 = jnp.bfloat16
MESH = pl.DeviceIdType.MESH


def split(value):
    high = value.astype(BF16)
    return high, (value - high.astype(F32)).astype(BF16)


def dot(a, b):
    return lax.dot_general(a, b, (((1,), (0,)), ((), ())), preferred_element_type=F32)


def split_dot(a_high, a_low, b_high, b_low):
    return dot(a_high, b_high) + (dot(a_high, b_low) + dot(a_low, b_high))


def kernel(parts, ranks, local_ref, seed_ref, band_ref, pattern_ref, out_ref, var_ref,
           nxt, odd, wbuf, m_high, m_low, loc, wc_high, wc_low, wt_high, wt_low,
           wsend, wrecv, nsend, nrecv, hsend, hrecv, rsend, rrecv, lsem):
    p, t = lax.axis_index("tm"), lax.axis_index("tile")
    rows, width = seed_ref.shape[1], seed_ref.shape[2]
    tr = wbuf.shape[3]
    lt = width // tr
    g = 2 if lt % 2 == 0 else 1
    span = (g + 2) * tr
    chunk = 256 if width % 256 == 0 else tr
    inner = pl.ds(tr, width)
    everything = pl.ds(0, width)
    has_next = p < parts - 1

    barrier = pltpu.get_barrier_semaphore()

    @pl.loop(0, ranks)
    def _(u):
        @pl.when(u != t)
        def _():
            pl.semaphore_signal(barrier, inc=1, device_id={"tile": u}, device_id_type=MESH)

    for a in (-1, 1):
        for b in (-1, 0, 1):
            @pl.when((p + a >= 0) & (p + a < parts) & (t + b >= 0) & (t + b < ranks))
            def _(a=a, b=b):
                pl.semaphore_signal(barrier, inc=1, device_id={"tm": p + a, "tile": t + b}, device_id_type=MESH)
    near_tm = jnp.where(p > 0, 1, 0) + jnp.where(p < parts - 1, 1, 0)
    near_tile = 1 + jnp.where(t > 0, 1, 0) + jnp.where(t < ranks - 1, 1, 0)
    pl.semaphore_wait(barrier, ranks - 1 + near_tm * near_tile)

    def block(u):
        return pl.ds(pl.multiple_of(u * width, width), width)

    def tile(b):
        return pl.ds(pl.multiple_of(b * tr, tr), tr)

    def triangle(s):
        behind, ahead = t - s, t + s
        count = ranks - 1 - t if s > 0 else t
        has_behind, has_ahead = (t > 0, t < ranks - 1) if s > 0 else (t < ranks - 1, t > 0)
        first, last = pl.ds(tr, tr), pl.ds(width, tr)
        left, right = pl.ds(0, tr), pl.ds(tr + width, tr)
        edge_behind, edge_ahead = (first, last) if s > 0 else (last, first)
        halo_behind, halo_ahead = (left, right) if s > 0 else (right, left)
        tile_behind, tile_ahead = (t * lt - 1, (t + 1) * lt) if s > 0 else ((t + 1) * lt, t * lt - 1)
        tile_corner = (t + 1) * lt - 1 if s > 0 else t * lt

        def groups(base, start, does, action):
            number = ranks - 1 - base if s > 0 else base

            @pl.when(does)
            def _():
                @pl.loop(start, number + 1)
                def _(k):
                    action(base + s * k)


        def w_copy(j, u):
            part = wbuf.at[j, pl.ds(u * lt * 3, lt * 3)]
            return pltpu.make_async_remote_copy(
                src_ref=part, dst_ref=part, send_sem=wsend.at[j, u], recv_sem=wrecv.at[j, u],
                device_id={"tile": behind}, device_id_type=MESH)

        def pass_on(j):
            def one(u):
                w_copy(j, u).wait_recv()
                w_copy(j, u).start()
            groups(t, 1, has_behind, one)

        def arrive(j, u):
            @pl.when(jnp.logical_not(has_behind))
            def _():
                w_copy(j, u).wait_recv()


        def seed_copy(src, dst, kind, u, target):
            return pltpu.make_async_remote_copy(
                src_ref=seed_ref.at[(0,) + src], dst_ref=nxt.at[dst],
                send_sem=nsend.at[kind, u], recv_sem=nrecv.at[kind, u],
                device_id={"tm": p - 1, "tile": target}, device_id_type=MESH)

        def seeds(action):
            low, high = pl.ds(0, tr), pl.ds(width - tr, tr)
            toward, back = (low, high) if s > 0 else (high, low)
            sends = p > 0
            number = t if s > 0 else ranks - 1 - t

            def walk(start, does, one):
                @pl.when(does)
                def _():
                    @pl.loop(start, number + 1)
                    def _(k):
                        one(t - s * k)

            walk(0, sends & has_ahead, lambda u: action(
                seed_copy((block(u), back), (block(u), halo_behind), 2, u, ahead)))
            walk(2, sends & has_behind, lambda u: action(
                seed_copy((block(u), toward), (block(u), halo_ahead), 1, u, behind)))

            @pl.when(sends & has_behind)
            def _():
                corner = tile(t * lt if s > 0 else (t + 1) * lt - 1)
                action(seed_copy((corner, toward), (corner, halo_ahead), 4, 0, behind))

            @pl.when(sends & has_ahead)
            def _():
                row = tile(tile_ahead)
                action(seed_copy((row, everything), (row, inner), 3, 0, t))
            walk(0, sends, lambda u: action(seed_copy((block(u), everything), (block(u), inner), 0, u, t)))

        def seed_arrived(dst, kind, u):
            pltpu.make_async_remote_copy(
                src_ref=nxt.at[dst], dst_ref=nxt.at[dst], send_sem=nsend.at[kind, u], recv_sem=nrecv.at[kind, u],
                device_id={"tile": behind}, device_id_type=MESH).wait_recv()

        def halo_copy(place, source, target_place, kind, u, target):
            return pltpu.make_async_remote_copy(
                src_ref=odd.at[place, source], dst_ref=odd.at[place, target_place],
                send_sem=hsend.at[kind, u], recv_sem=hrecv.at[kind, u],
                device_id={"tile": target}, device_id_type=MESH)

        def halo_ahead_copy(u):
            return halo_copy(block(u), edge_ahead, halo_behind, 0, u, ahead)

        def halo_corner_copy(b):
            return halo_copy(tile(b), edge_ahead, halo_behind, 2, 0, ahead)

        def halo_behind_copy(u):
            return halo_copy(block(u), edge_behind, halo_ahead, 1, u, behind)

        def result_copy(u):
            return pltpu.make_async_remote_copy(
                src_ref=nxt.at[block(u), inner], dst_ref=out_ref.at[block(t), everything],
                send_sem=rsend.at[u], recv_sem=rrecv.at[t],
                device_id={"tile": u}, device_id_type=MESH)

        def result_arrived(u):
            pltpu.make_async_remote_copy(
                src_ref=nxt.at[block(u), inner], dst_ref=out_ref.at[block(u), everything],
                send_sem=rsend.at[u], recv_sem=rrecv.at[u],
                device_id={"tile": behind}, device_id_type=MESH).wait_recv()

        def clear_halo(field, does):
            for missing, place in ((has_behind, halo_behind), (has_ahead, halo_ahead)):
                @pl.when(jnp.logical_not(missing) & does)
                def _(place=place):
                    field[:, place] = jnp.zeros((rows, tr), F32)

        def own_tile(i):
            return tile(t * lt + i)

        def mirror_ahead(field):
            @pl.when(has_ahead)
            def _():
                for i in range(lt):
                    field[own_tile(i), halo_ahead] = field[tile(tile_ahead), pl.ds(tr + i * tr, tr)].T

            @pl.when(has_ahead & has_behind)
            def _():
                field[tile(tile_behind), halo_ahead] = field[tile(tile_ahead), halo_behind].T

        def column_product(field, j):
            for i in range(lt // g):
                for c in range(g):
                    for k in range(3):
                        high, low = split(wbuf[j, (t * lt + i * g + c) * 3 + k])
                        at = (i, pl.ds((c + k) * tr, tr), pl.ds(c * tr, tr))
                        wc_high[at] = high
                        wc_low[at] = low

            def some_rows(start, size):
                for i in range(lt // g):
                    high, low = split(field[pl.ds(start, size), pl.ds(i * g * tr, span)])
                    value = split_dot(high, low, wc_high[i], wc_low[i])
                    at = (pl.ds(pl.multiple_of(start + tr, tr), size), pl.ds(i * g * tr, g * tr))
                    high, low = split(value)
                    m_high[at] = high
                    m_low[at] = low

            @pl.when(has_behind)
            def _():
                some_rows(pl.multiple_of(tile_behind * tr, tr), tr)

            base = t * width if s > 0 else 0

            @pl.loop(0, (count + 1) * (width // chunk))
            def _(r):
                some_rows(pl.multiple_of(base + r * chunk, chunk), chunk)

        def left_rows(j, owner, target, columns, turned):
            @pl.loop(0, lt // g)
            def _(i):
                begin = owner * lt + i * g
                for c in range(g):
                    for k in range(3):
                        high, low = split(wbuf[j, (begin + c) * 3 + k].T)
                        at = (pl.ds(c * tr, tr), pl.ds((c + k) * tr, tr))
                        wt_high[at] = high
                        wt_low[at] = low
                start = pl.multiple_of(begin * tr, tr)
                source = pl.ds(start, span)
                value = split_dot(wt_high[...], wt_low[...], m_high[source, :], m_low[source, :])
                place = pl.ds(start, g * tr)
                value = loc[j, place, :].astype(F32) + value
                target[place, columns] = value
                if turned:
                    for c in range(g):
                        lanes = pl.ds(pl.multiple_of(tr + (i * g + c) * tr, tr), tr)
                        for q in range(lt):
                            nxt[tile(owner * lt + q), lanes] = value[c * tr:(c + 1) * tr, q * tr:(q + 1) * tr].T

        def diagonal(index, field, offset):
            eye = lax.broadcasted_iota(jnp.int32, (tr, tr), 0) == lax.broadcasted_iota(jnp.int32, (tr, tr), 1)
            for c in range(lt):
                part = field[own_tile(c), pl.ds(offset + c * tr, tr)]
                var_ref[pl.ds(index, 1), pl.ds(c * tr, tr)] = jnp.sum(jnp.where(eye, part, 0.0), axis=0, keepdims=True)

        own_local = [pltpu.make_async_copy(band_ref.at[j], wbuf.at[j, pl.ds(t * lt * 3, lt * 3)], lsem.at[j]) for j in (0, 1)]
        locals_in = pltpu.make_async_copy(local_ref, loc, lsem.at[2])
        for copy in own_local[::-1]:
            copy.start()
        seeds(lambda copy: copy.start())
        locals_in.start()

        def own_factor(j):
            own_local[j].wait()
            for b in range(lt):
                for k in range(3):
                    at = (j, (t * lt + b) * 3 + k)
                    wbuf[at] = wbuf[at] * pattern_ref[k, j, b].astype(F32)

        own_factor(1)

        @pl.when(has_behind)
        def _():
            w_copy(1, t).start()

        own_factor(0)
        clear_halo(odd, True)
        clear_halo(nxt, has_next)

        @pl.when(p == parts - 1)
        def _():
            nxt[...] = jnp.zeros_like(nxt)

        for ref in (m_high, m_low):
            ref[pl.ds(0, tr), :] = jnp.zeros((tr, width), BF16)
            ref[pl.ds(tr + rows, tr), :] = jnp.zeros((tr, width), BF16)
        for ref in (wc_high, wc_low, wt_high, wt_low):
            ref[...] = jnp.zeros_like(ref)

        pass_on(1)

        @pl.when(has_behind)
        def _():
            w_copy(0, t).start()

        if s < 0:
            pass_on(0)

        groups(t, 1, has_next & has_behind, lambda u: seed_arrived((block(u), halo_behind), 1, u))
        groups(t, 1, has_next & has_ahead, lambda u: seed_arrived((block(u), halo_ahead), 2, u))

        @pl.when(has_next & has_behind)
        def _():
            seed_arrived((tile(tile_behind), halo_behind), 4, 0)
            seed_arrived((tile(tile_behind), inner), 3, 0)
        groups(t, 0, has_next, lambda u: seed_arrived((block(u), inner), 0, u))

        @pl.when(has_behind)
        def _():
            for i in range(lt):
                nxt[own_tile(i), halo_behind] = nxt[tile(tile_behind), pl.ds(tr + i * tr, tr)].T
        mirror_ahead(nxt)
        column_product(nxt, 1)
        locals_in.wait()
        left_rows(1, t, odd, inner, False)

        def odd_rows(u):
            arrive(1, u)
            left_rows(1, u, odd, inner, False)
        groups(t, 1, True, odd_rows)

        groups(t, 0, has_behind, lambda u: halo_behind_copy(u).start())

        @pl.when(has_ahead)
        def _():
            halo_corner_copy(tile_corner).start()
        groups(t, 1, has_ahead, lambda u: halo_ahead_copy(u).start())
        if s > 0:
            pass_on(0)
        diagonal(1, odd, tr)
        mirror_ahead_own = has_ahead

        @pl.when(has_behind)
        def _():
            halo_corner_copy(tile_behind).wait_recv()
        groups(t, 0, has_behind, lambda u: halo_ahead_copy(u).wait_recv())
        groups(t, 1, has_ahead, lambda u: halo_behind_copy(u).wait_recv())

        @pl.when(has_behind)
        def _():
            for i in range(lt):
                odd[tile(tile_behind), pl.ds(tr + i * tr, tr)] = odd[own_tile(i), halo_behind].T
        mirror_ahead(odd)
        column_product(odd, 0)
        left_rows(0, t, out_ref, everything, False)
        diagonal(0, out_ref, 0)

        def first_rows(u):
            arrive(0, u)
            left_rows(0, u, out_ref, everything, True)
            result_copy(u).start()
        groups(t, 1, True, first_rows)

        @pl.when(has_behind)
        def _():
            @pl.loop(1, ranks - count)
            def _(k):
                result_arrived(t - s * k)

        for j in (1, 0):
            groups(t, 0, has_behind, lambda u, j=j: w_copy(j, u).wait_send())
        seeds(lambda copy: copy.wait_send())
        groups(t, 0, has_behind, lambda u: halo_behind_copy(u).wait_send())

        @pl.when(has_ahead)
        def _():
            halo_corner_copy(tile_corner).wait_send()
        groups(t, 1, has_ahead, lambda u: halo_ahead_copy(u).wait_send())
        groups(t, 1, True, lambda u: result_copy(u).wait_send())

    for remainder, s in ((0, 1), (1, -1)):
        @pl.when(lax.rem(p, 2) == remainder)
        def _(s=s):
            triangle(s)


def per_device(parts, ranks, local_inv, seed_inv, band, pattern):
    rows, width = seed_inv.shape[1:]
    lt, tr = band.shape[1], band.shape[3]
    tiles = rows // tr
    g = 2 if lt % 2 == 0 else 1
    span = (g + 2) * tr
    dma = pltpu.SemaphoreType.DMA
    out, var = pl.pallas_call(
        functools.partial(kernel, parts, ranks),
        out_shape=(pltpu.VMEM((rows, width), F32), pltpu.VMEM((2, width), F32)),
        in_specs=[pl.BlockSpec(memory_space=pltpu.HBM)] * 3 + [pl.BlockSpec(memory_space=pltpu.SMEM)],
        out_specs=(pl.BlockSpec(memory_space=pltpu.VMEM), pl.BlockSpec(memory_space=pltpu.VMEM)),
        scratch_shapes=[
            pltpu.VMEM((rows, width + 2 * tr), F32),
            pltpu.VMEM((rows, width + 2 * tr), F32),
            pltpu.VMEM((2, tiles * 3, tr, tr), F32),
            pltpu.VMEM((rows + 2 * tr, width), BF16),
            pltpu.VMEM((rows + 2 * tr, width), BF16),
            pltpu.VMEM((2, rows, width), BF16),
            pltpu.VMEM((lt // g, span, g * tr), BF16),
            pltpu.VMEM((lt // g, span, g * tr), BF16),
            pltpu.VMEM((g * tr, span), BF16),
            pltpu.VMEM((g * tr, span), BF16),
            dma((2, ranks)),
            dma((2, ranks)),
            dma((5, ranks)),
            dma((5, ranks)),
            dma((3, ranks)),
            dma((3, ranks)),
            dma((ranks,)),
            dma((ranks,)),
            dma((3,)),
        ],
        compiler_params=pltpu.CompilerParams(
            collective_id=0, has_side_effects=True, vmem_limit_bytes=58 * 1024 * 1024
        ),
    )(local_inv, seed_inv, band.reshape(2, lt * 3, tr, tr), pattern.transpose(2, 0, 1))
    return out[None], var


def solution(mesh):
    placed = (
        P("tm", None, "tile"),
        P("tm", None, "tile"),
        P("tm", "tile", None, None, None),
        P("tm", "tile", None),
    )
    return jax.shard_map(
        functools.partial(per_device, mesh.shape["tm"], mesh.shape["tile"]),
        mesh=mesh,
        in_specs=placed,
        out_specs=(P("tm", None, "tile"), P("tm", "tile")),
        check_vma=False,
    )
```

```python
import functools

import jax
import jax.numpy as jnp
from jax import lax
from jax.experimental import pallas as pl
from jax.experimental.pallas import tpu as pltpu
from jax.sharding import PartitionSpec as P

F32 = jnp.float32
BF16 = jnp.bfloat16
MESH = pl.DeviceIdType.MESH


def split(value):
    high = value.astype(BF16)
    return high, (value - high.astype(F32)).astype(BF16)


def dot(a, b):
    return lax.dot_general(a, b, (((1,), (0,)), ((), ())), preferred_element_type=F32)


def split_dot(a_high, a_low, b_high, b_low):
    return dot(a_high, b_high) + (dot(a_high, b_low) + dot(a_low, b_high))


def kernel(parts, ranks, local_ref, seed_ref, band_ref, pattern_ref, out_ref, var_ref,
           nxt, odd, wbuf, m_high, m_low, loc, wc_high, wc_low, wt_high, wt_low,
           wsend, wrecv, nsend, nrecv, hsend, hrecv, rsend, rrecv, lsem, go):
    p, t = lax.axis_index("tm"), lax.axis_index("tile")
    rows, width = seed_ref.shape[1], seed_ref.shape[2]
    tr = wbuf.shape[3]
    lt = width // tr
    g = 2 if lt % 2 == 0 else 1
    span = (g + 2) * tr
    chunk = 256 if width % 256 == 0 else tr
    inner = pl.ds(tr, width)
    everything = pl.ds(0, width)
    has_next = p < parts - 1

    barrier = pltpu.get_barrier_semaphore()

    paired = parts % 2 == 0
    partner = p + 1 - 2 * lax.rem(p, 2)

    def greet(q, u):
        pl.semaphore_signal(barrier, inc=1, device_id={"tm": q, "tile": u}, device_id_type=MESH)

    @pl.loop(0, ranks)
    def _(u):
        @pl.when(u != t)
        def _():
            greet(p, u)
        if paired:
            greet(partner, u)

    for a in (-1, 1):
        for b in (-1, 0, 1):
            meet = (p + a >= 0) & (p + a < parts) & (t + b >= 0) & (t + b < ranks)

            @pl.when(meet & (p + a != partner) if paired else meet)
            def _(a=a, b=b):
                greet(p + a, t + b)
    near_tm = jnp.where(p > 0, 1, 0) + jnp.where(p < parts - 1, 1, 0) - (1 if paired else 0)
    near_tile = 1 + jnp.where(t > 0, 1, 0) + jnp.where(t < ranks - 1, 1, 0)
    meets = ranks - 1 + (ranks if paired else 0) + near_tm * near_tile
    own_local = [pltpu.make_async_copy(band_ref.at[j], wbuf.at[j, pl.ds(t * lt * 3, lt * 3)], lsem.at[j]) for j in (0, 1)]
    locals_in = pltpu.make_async_copy(local_ref, loc, lsem.at[2])
    for copy in own_local[::-1]:
        copy.start()
    locals_in.start()

    @pl.when(p == parts - 1)
    def _():
        nxt[...] = jnp.zeros_like(nxt)

    for ref in (m_high, m_low):
        ref[pl.ds(0, tr), :] = jnp.zeros((tr, width), BF16)
        ref[pl.ds(tr + rows, tr), :] = jnp.zeros((tr, width), BF16)
    for ref in (wc_high, wc_low, wt_high, wt_low):
        ref[...] = jnp.zeros_like(ref)
    for j in (1, 0):
        own_local[j].wait()
        for b in range(lt):
            for k in range(3):
                at = (j, (t * lt + b) * 3 + k)
                wbuf[at] = wbuf[at] * pattern_ref[k, j, b].astype(F32)
    pl.semaphore_wait(barrier, meets)

    def block(u):
        return pl.ds(pl.multiple_of(u * width, width), width)

    def tile(b):
        return pl.ds(pl.multiple_of(b * tr, tr), tr)

    def triangle(s):
        behind, ahead = t - s, t + s
        count = ranks - 1 - t if s > 0 else t
        has_behind, has_ahead = (t > 0, t < ranks - 1) if s > 0 else (t < ranks - 1, t > 0)
        first, last = pl.ds(tr, tr), pl.ds(width, tr)
        left, right = pl.ds(0, tr), pl.ds(tr + width, tr)
        edge_behind, edge_ahead = (first, last) if s > 0 else (last, first)
        halo_behind, halo_ahead = (left, right) if s > 0 else (right, left)
        tile_behind, tile_ahead = (t * lt - 1, (t + 1) * lt) if s > 0 else ((t + 1) * lt, t * lt - 1)
        tile_corner = (t + 1) * lt - 1 if s > 0 else t * lt

        def groups(base, start, does, action):
            number = ranks - 1 - base if s > 0 else base

            @pl.when(does)
            def _():
                @pl.loop(start, number + 1)
                def _(k):
                    action(base + s * k)


        def w_copy(j, u):
            part = wbuf.at[j, pl.ds(u * lt * 3, lt * 3)]
            return pltpu.make_async_remote_copy(
                src_ref=part, dst_ref=part, send_sem=wsend.at[j, u], recv_sem=wrecv.at[j, u],
                device_id={"tile": behind}, device_id_type=MESH)

        def pass_one(j, u):
            w_copy(j, u).wait_recv()
            w_copy(j, u).start()

        def pass_on(j):
            groups(t, 1, has_behind, lambda u: pass_one(j, u))

        def arrive(j, u):
            @pl.when(jnp.logical_not(has_behind))
            def _():
                w_copy(j, u).wait_recv()


        def seed_copy(src, dst, kind, u, target):
            return pltpu.make_async_remote_copy(
                src_ref=seed_ref.at[(0,) + src], dst_ref=nxt.at[dst],
                send_sem=nsend.at[kind, u], recv_sem=nrecv.at[kind, u],
                device_id={"tm": p - 1, "tile": target}, device_id_type=MESH)

        def seeds(action):
            low, high = pl.ds(0, tr), pl.ds(width - tr, tr)
            toward, back = (low, high) if s > 0 else (high, low)
            sends = p > 0
            number = t if s > 0 else ranks - 1 - t

            def walk(start, does, one):
                @pl.when(does)
                def _():
                    @pl.loop(start, number + 1)
                    def _(k):
                        one(t - s * k)

            walk(0, sends & has_ahead, lambda u: action(
                seed_copy((block(u), back), (block(u), halo_behind), 2, u, ahead)))
            walk(2, sends & has_behind, lambda u: action(
                seed_copy((block(u), toward), (block(u), halo_ahead), 1, u, behind)))

            @pl.when(sends & has_behind)
            def _():
                corner = tile(t * lt if s > 0 else (t + 1) * lt - 1)
                action(seed_copy((corner, toward), (corner, halo_ahead), 4, 0, behind))

            @pl.when(sends & has_ahead)
            def _():
                row = tile(tile_ahead)
                action(seed_copy((row, everything), (row, inner), 3, 0, t))
            walk(0, sends, lambda u: action(seed_copy((block(u), everything), (block(u), inner), 0, u, t)))

        def seed_arrived(dst, kind, u):
            pltpu.make_async_remote_copy(
                src_ref=nxt.at[dst], dst_ref=nxt.at[dst], send_sem=nsend.at[kind, u], recv_sem=nrecv.at[kind, u],
                device_id={"tile": behind}, device_id_type=MESH).wait_recv()

        def halo_copy(place, source, target_place, kind, u, target):
            return pltpu.make_async_remote_copy(
                src_ref=odd.at[place, source], dst_ref=odd.at[place, target_place],
                send_sem=hsend.at[kind, u], recv_sem=hrecv.at[kind, u],
                device_id={"tile": target}, device_id_type=MESH)

        def halo_ahead_copy(u):
            return halo_copy(block(u), edge_ahead, halo_behind, 0, u, ahead)

        def halo_corner_copy(b):
            return halo_copy(tile(b), edge_ahead, halo_behind, 2, 0, ahead)

        def halo_behind_copy(u):
            return halo_copy(block(u), edge_behind, halo_ahead, 1, u, behind)

        def result_copy(u):
            return pltpu.make_async_remote_copy(
                src_ref=nxt.at[block(u), inner], dst_ref=out_ref.at[block(t), everything],
                send_sem=rsend.at[u], recv_sem=rrecv.at[t],
                device_id={"tile": u}, device_id_type=MESH)

        def result_arrived(u):
            pltpu.make_async_remote_copy(
                src_ref=nxt.at[block(u), inner], dst_ref=out_ref.at[block(u), everything],
                send_sem=rsend.at[u], recv_sem=rrecv.at[u],
                device_id={"tile": behind}, device_id_type=MESH).wait_recv()

        def signal_partner():
            if paired:
                @pl.loop(0, ranks)
                def _(u):
                    @pl.when(u != t)
                    def _():
                        pl.semaphore_signal(go, inc=1, device_id={"tm": partner, "tile": u}, device_id_type=MESH)

        def wait_partner():
            if paired:
                pl.semaphore_wait(go, 1)

        def clear_halo(field, does):
            for missing, place in ((has_behind, halo_behind), (has_ahead, halo_ahead)):
                @pl.when(jnp.logical_not(missing) & does)
                def _(place=place):
                    field[:, place] = jnp.zeros((rows, tr), F32)

        def own_tile(i):
            return tile(t * lt + i)

        def mirror_ahead(field):
            @pl.when(has_ahead)
            def _():
                for i in range(lt):
                    field[own_tile(i), halo_ahead] = field[tile(tile_ahead), pl.ds(tr + i * tr, tr)].T

            @pl.when(has_ahead & has_behind)
            def _():
                field[tile(tile_behind), halo_ahead] = field[tile(tile_ahead), halo_behind].T

        def own_columns(j):
            for i in range(lt // g):
                for c in range(g):
                    for k in range(3):
                        high, low = split(wbuf[j, (t * lt + i * g + c) * 3 + k])
                        at = (i, pl.ds((c + k) * tr, tr), pl.ds(c * tr, tr))
                        wc_high[at] = high
                        wc_low[at] = low

        def some_rows(field, start, size):
            for i in range(lt // g):
                high, low = split(field[pl.ds(start, size), pl.ds(i * g * tr, span)])
                value = split_dot(high, low, wc_high[i], wc_low[i])
                at = (pl.ds(pl.multiple_of(start + tr, tr), size), pl.ds(i * g * tr, g * tr))
                high, low = split(value)
                m_high[at] = high
                m_low[at] = low

        def group_rows(field, u):
            @pl.loop(0, width // chunk)
            def _(r):
                some_rows(field, pl.multiple_of(u * width + r * chunk, chunk), chunk)

        def near_rows(field):
            @pl.when(has_behind)
            def _():
                some_rows(field, pl.multiple_of(tile_behind * tr, tr), tr)
            group_rows(field, t)

        def left_rows(j, owner, target, columns, turned):
            @pl.loop(0, lt // g)
            def _(i):
                begin = owner * lt + i * g
                for c in range(g):
                    for k in range(3):
                        high, low = split(wbuf[j, (begin + c) * 3 + k].T)
                        at = (pl.ds(c * tr, tr), pl.ds((c + k) * tr, tr))
                        wt_high[at] = high
                        wt_low[at] = low
                start = pl.multiple_of(begin * tr, tr)
                source = pl.ds(start, span)
                value = split_dot(wt_high[...], wt_low[...], m_high[source, :], m_low[source, :])
                place = pl.ds(start, g * tr)
                value = loc[j, place, :].astype(F32) + value
                target[place, columns] = value
                if turned:
                    for c in range(g):
                        lanes = pl.ds(pl.multiple_of(tr + (i * g + c) * tr, tr), tr)
                        for q in range(lt):
                            nxt[tile(owner * lt + q), lanes] = value[c * tr:(c + 1) * tr, q * tr:(q + 1) * tr].T

        def diagonal(index, field, offset):
            eye = lax.broadcasted_iota(jnp.int32, (tr, tr), 0) == lax.broadcasted_iota(jnp.int32, (tr, tr), 1)
            for c in range(lt):
                part = field[own_tile(c), pl.ds(offset + c * tr, tr)]
                var_ref[pl.ds(index, 1), pl.ds(c * tr, tr)] = jnp.sum(jnp.where(eye, part, 0.0), axis=0, keepdims=True)

        far_end = t + s * count

        @pl.when(has_behind)
        def _():
            w_copy(1, t).start()
        seeds(lambda copy: copy.start())
        clear_halo(odd, True)
        clear_halo(nxt, has_next)
        pass_on(1)

        @pl.when(has_behind)
        def _():
            w_copy(0, t).start()

        def seeds_here(u):
            @pl.when(has_next)
            def _():
                seed_arrived((block(u), inner), 0, u)
                seed_arrived((block(u), halo_ahead), 2, u)

            @pl.when(has_next & has_behind)
            def _():
                seed_arrived((block(u), halo_behind), 1, u)

        @pl.when(has_next)
        def _():
            seed_arrived((block(t), inner), 0, t)

        @pl.when(has_next & has_behind)
        def _():
            seed_arrived((tile(tile_behind), inner), 3, 0)
            seed_arrived((tile(tile_behind), halo_behind), 4, 0)

        @pl.when(has_ahead)
        def _():
            seeds_here(ahead)

        @pl.when(has_behind)
        def _():
            for i in range(lt):
                nxt[own_tile(i), halo_behind] = nxt[tile(tile_behind), pl.ds(tr + i * tr, tr)].T
        mirror_ahead(nxt)
        own_columns(1)
        near_rows(nxt)
        locals_in.wait()

        def odd_rows(u):
            @pl.when(u != t)
            def _():
                arrive(1, u)
            left_rows(1, u, odd, inner, False)

            @pl.when(has_behind)
            def _():
                halo_behind_copy(u).start()

            @pl.when(has_ahead & (u == t))
            def _():
                halo_corner_copy(tile_corner).start()

            @pl.when(u != t)
            def _():
                halo_ahead_copy(u).start()

        def odd_step(u):
            if s < 0:
                @pl.when(has_behind)
                def _():
                    pass_one(0, u)

            @pl.when(u != ahead)
            def _():
                seeds_here(u)
            group_rows(nxt, u)
            odd_rows(u - s)
        groups(t, 1, has_ahead, odd_step)
        odd_rows(far_end)
        if s > 0:
            pass_on(0)
        diagonal(1, odd, tr)

        def halos_here(u):
            halo_behind_copy(u).wait_recv()

            @pl.when(has_behind)
            def _():
                halo_ahead_copy(u).wait_recv()

        @pl.when(has_behind)
        def _():
            halo_corner_copy(tile_behind).wait_recv()
            halo_ahead_copy(t).wait_recv()

        @pl.when(has_ahead)
        def _():
            halos_here(ahead)

        @pl.when(has_behind)
        def _():
            for i in range(lt):
                odd[tile(tile_behind), pl.ds(tr + i * tr, tr)] = odd[own_tile(i), halo_behind].T
        mirror_ahead(odd)
        own_columns(0)
        near_rows(odd)

        def first_rows(u):
            arrive(0, u)
            left_rows(0, u, out_ref, everything, True)

        def first_step(u):
            @pl.when(u != ahead)
            def _():
                halos_here(u)
            group_rows(odd, u)

            @pl.when(u == ahead)
            def _():
                left_rows(0, t, out_ref, everything, False)

            @pl.when(u != ahead)
            def _():
                first_rows(u - s)
                result_copy(u - s).start()
        groups(t, 1, has_ahead, first_step)

        @pl.when(has_ahead)
        def _():
            arrive(0, far_end)

            @pl.when(jnp.logical_not(has_behind))
            def _():
                signal_partner()
            left_rows(0, far_end, out_ref, everything, True)
            wait_partner()
            result_copy(far_end).start()

        @pl.when(jnp.logical_not(has_ahead))
        def _():
            left_rows(0, t, out_ref, everything, False)
        diagonal(0, out_ref, 0)

        @pl.when(has_behind)
        def _():
            @pl.loop(1, ranks - count)
            def _(k):
                result_arrived(t - s * k)

        for j in (1, 0):
            groups(t, 0, has_behind, lambda u, j=j: w_copy(j, u).wait_send())
        seeds(lambda copy: copy.wait_send())
        groups(t, 0, has_behind, lambda u: halo_behind_copy(u).wait_send())

        @pl.when(has_ahead)
        def _():
            halo_corner_copy(tile_corner).wait_send()
        groups(t, 1, has_ahead, lambda u: halo_ahead_copy(u).wait_send())
        groups(t, 1, True, lambda u: result_copy(u).wait_send())

    for remainder, s in ((0, 1), (1, -1)):
        @pl.when(lax.rem(p, 2) == remainder)
        def _(s=s):
            triangle(s)


def per_device(parts, ranks, local_inv, seed_inv, band, pattern):
    rows, width = seed_inv.shape[1:]
    lt, tr = band.shape[1], band.shape[3]
    tiles = rows // tr
    g = 2 if lt % 2 == 0 else 1
    span = (g + 2) * tr
    dma = pltpu.SemaphoreType.DMA
    out, var = pl.pallas_call(
        functools.partial(kernel, parts, ranks),
        out_shape=(pltpu.VMEM((rows, width), F32), pltpu.VMEM((2, width), F32)),
        in_specs=[pl.BlockSpec(memory_space=pltpu.HBM)] * 3 + [pl.BlockSpec(memory_space=pltpu.SMEM)],
        out_specs=(pl.BlockSpec(memory_space=pltpu.VMEM), pl.BlockSpec(memory_space=pltpu.VMEM)),
        scratch_shapes=[
            pltpu.VMEM((rows, width + 2 * tr), F32),
            pltpu.VMEM((rows, width + 2 * tr), F32),
            pltpu.VMEM((2, tiles * 3, tr, tr), F32),
            pltpu.VMEM((rows + 2 * tr, width), BF16),
            pltpu.VMEM((rows + 2 * tr, width), BF16),
            pltpu.VMEM((2, rows, width), BF16),
            pltpu.VMEM((lt // g, span, g * tr), BF16),
            pltpu.VMEM((lt // g, span, g * tr), BF16),
            pltpu.VMEM((g * tr, span), BF16),
            pltpu.VMEM((g * tr, span), BF16),
            dma((2, ranks)),
            dma((2, ranks)),
            dma((5, ranks)),
            dma((5, ranks)),
            dma((3, ranks)),
            dma((3, ranks)),
            dma((ranks,)),
            dma((ranks,)),
            dma((3,)),
            pltpu.SemaphoreType.REGULAR,
        ],
        compiler_params=pltpu.CompilerParams(
            collective_id=0, has_side_effects=True, vmem_limit_bytes=58 * 1024 * 1024
        ),
    )(local_inv, seed_inv, band.reshape(2, lt * 3, tr, tr), pattern.transpose(2, 0, 1))
    return out[None], var


def solution(mesh):
    placed = (
        P("tm", None, "tile"),
        P("tm", None, "tile"),
        P("tm", "tile", None, None, None),
        P("tm", "tile", None),
    )
    return jax.shard_map(
        functools.partial(per_device, mesh.shape["tm"], mesh.shape["tile"]),
        mesh=mesh,
        in_specs=placed,
        out_specs=(P("tm", None, "tile"), P("tm", "tile")),
        check_vma=False,
    )
```

```python
import functools

import jax
import jax.numpy as jnp
from jax import lax
from jax.experimental import pallas as pl
from jax.experimental.pallas import tpu as pltpu
from jax.sharding import PartitionSpec as P

F32 = jnp.float32
BF16 = jnp.bfloat16
MESH = pl.DeviceIdType.MESH


def split(value):
    high = value.astype(BF16)
    return high, (value - high.astype(F32)).astype(BF16)


def dot(a, b):
    return lax.dot_general(a, b, (((1,), (0,)), ((), ())), preferred_element_type=F32)


def split_dot(a_high, a_low, b_high, b_low):
    return dot(a_high, b_high) + (dot(a_high, b_low) + dot(a_low, b_high))


def kernel(parts, ranks, local_ref, seed_ref, band_ref, pattern_ref, out_ref, var_ref,
           nxt, odd, wbuf, m_high, m_low, loc, wc_high, wc_low, wt_high, wt_low,
           wsend, wrecv, nsend, nrecv, hsend, hrecv, rsend, rrecv, lsem, go):
    p, t = lax.axis_index("tm"), lax.axis_index("tile")
    rows, width = seed_ref.shape[1], seed_ref.shape[2]
    tr = wbuf.shape[3]
    lt = width // tr
    g = 2 if lt % 2 == 0 else 1
    span = (g + 2) * tr
    chunk = 256 if width % 256 == 0 else tr
    inner = pl.ds(tr, width)
    everything = pl.ds(0, width)
    has_next = p < parts - 1

    barrier = pltpu.get_barrier_semaphore()

    paired = parts % 2 == 0
    partner = p + 1 - 2 * lax.rem(p, 2)

    def greet(q, u):
        pl.semaphore_signal(barrier, inc=1, device_id={"tm": q, "tile": u}, device_id_type=MESH)

    @pl.loop(0, ranks)
    def _(u):
        @pl.when(u != t)
        def _():
            greet(p, u)
        if paired:
            greet(partner, u)

    for a in (-1, 1):
        for b in (-1, 0, 1):
            meet = (p + a >= 0) & (p + a < parts) & (t + b >= 0) & (t + b < ranks)

            @pl.when(meet & (p + a != partner) if paired else meet)
            def _(a=a, b=b):
                greet(p + a, t + b)
    near_tm = jnp.where(p > 0, 1, 0) + jnp.where(p < parts - 1, 1, 0) - (1 if paired else 0)
    near_tile = 1 + jnp.where(t > 0, 1, 0) + jnp.where(t < ranks - 1, 1, 0)
    meets = ranks - 1 + (ranks if paired else 0) + near_tm * near_tile
    own_local = [pltpu.make_async_copy(band_ref.at[j], wbuf.at[j, pl.ds(t * lt * 3, lt * 3)], lsem.at[j]) for j in (0, 1)]
    locals_in = pltpu.make_async_copy(local_ref, loc, lsem.at[2])
    for copy in own_local[::-1]:
        copy.start()
    locals_in.start()

    @pl.when(p == parts - 1)
    def _():
        nxt[...] = jnp.zeros_like(nxt)

    for ref in (m_high, m_low):
        for j in (0, 1):
            ref[j, pl.ds(0, tr), :] = jnp.zeros((tr, width), BF16)
            ref[j, pl.ds(tr + rows, tr), :] = jnp.zeros((tr, width), BF16)
    for ref in (wc_high, wc_low, wt_high, wt_low):
        ref[...] = jnp.zeros_like(ref)
    for j in (1, 0):
        own_local[j].wait()
        for b in range(lt):
            for k in range(3):
                at = (j, (t * lt + b) * 3 + k)
                wbuf[at] = wbuf[at] * pattern_ref[k, j, b].astype(F32)
    pl.semaphore_wait(barrier, meets)

    def block(u):
        return pl.ds(pl.multiple_of(u * width, width), width)

    def tile(b):
        return pl.ds(pl.multiple_of(b * tr, tr), tr)

    def triangle(s):
        behind, ahead = t - s, t + s
        count = ranks - 1 - t if s > 0 else t
        has_behind, has_ahead = (t > 0, t < ranks - 1) if s > 0 else (t < ranks - 1, t > 0)
        first, last = pl.ds(tr, tr), pl.ds(width, tr)
        left, right = pl.ds(0, tr), pl.ds(tr + width, tr)
        edge_behind, edge_ahead = (first, last) if s > 0 else (last, first)
        halo_behind, halo_ahead = (left, right) if s > 0 else (right, left)
        tile_behind, tile_ahead = (t * lt - 1, (t + 1) * lt) if s > 0 else ((t + 1) * lt, t * lt - 1)
        tile_corner = (t + 1) * lt - 1 if s > 0 else t * lt

        def groups(base, start, does, action):
            number = ranks - 1 - base if s > 0 else base

            @pl.when(does)
            def _():
                @pl.loop(start, number + 1)
                def _(k):
                    action(base + s * k)


        def w_copy(j, u):
            part = wbuf.at[j, pl.ds(u * lt * 3, lt * 3)]
            return pltpu.make_async_remote_copy(
                src_ref=part, dst_ref=part, send_sem=wsend.at[j, u], recv_sem=wrecv.at[j, u],
                device_id={"tile": behind}, device_id_type=MESH)

        def pass_one(j, u):
            w_copy(j, u).wait_recv()
            w_copy(j, u).start()

        def pass_on(j):
            groups(t, 1, has_behind, lambda u: pass_one(j, u))

        def arrive(j, u):
            @pl.when(jnp.logical_not(has_behind))
            def _():
                w_copy(j, u).wait_recv()


        def seed_copy(src, dst, kind, u, target):
            return pltpu.make_async_remote_copy(
                src_ref=seed_ref.at[(0,) + src], dst_ref=nxt.at[dst],
                send_sem=nsend.at[kind, u], recv_sem=nrecv.at[kind, u],
                device_id={"tm": p - 1, "tile": target}, device_id_type=MESH)

        def lead(u, direction):
            return tile(u * lt if direction > 0 else (u + 1) * lt - 1)

        def rest(u, direction):
            return pl.ds(pl.multiple_of(u * width + (tr if direction > 0 else 0), tr), width - tr)

        def seeds(action):
            low, high = pl.ds(0, tr), pl.ds(width - tr, tr)
            toward, back = (low, high) if s > 0 else (high, low)
            number = t if s > 0 else ranks - 1 - t

            def pieces(u, source, place, kind, target):
                action(seed_copy((lead(u, -s), source), (lead(u, -s), place), kind + 5, u, target))
                if lt > 1:
                    action(seed_copy((rest(u, -s), source), (rest(u, -s), place), kind, u, target))

            @pl.when(p > 0)
            def _():
                @pl.when(has_ahead)
                def _():
                    row = tile(tile_ahead)
                    action(seed_copy((row, everything), (row, inner), 3, 0, t))

                @pl.when(has_behind)
                def _():
                    corner = tile(t * lt if s > 0 else (t + 1) * lt - 1)
                    action(seed_copy((corner, toward), (corner, halo_ahead), 4, 0, behind))
                action(seed_copy((block(t), everything), (block(t), inner), 0, t, t))

                @pl.when(has_ahead)
                def _():
                    pieces(t, back, halo_behind, 2, ahead)

                @pl.loop(1, number + 1)
                def _(k):
                    u = t - s * k
                    pieces(u, everything, inner, 0, t)

                    @pl.when(has_ahead)
                    def _():
                        pieces(u, back, halo_behind, 2, ahead)

                    @pl.when(k > 1)
                    def _():
                        pieces(u, toward, halo_ahead, 1, behind)

        def seed_arrived(dst, kind, u):
            pltpu.make_async_remote_copy(
                src_ref=nxt.at[dst], dst_ref=nxt.at[dst], send_sem=nsend.at[kind, u], recv_sem=nrecv.at[kind, u],
                device_id={"tile": behind}, device_id_type=MESH).wait_recv()

        def halo_copy(place, source, target_place, kind, u, target):
            return pltpu.make_async_remote_copy(
                src_ref=odd.at[place, source], dst_ref=odd.at[place, target_place],
                send_sem=hsend.at[kind, u], recv_sem=hrecv.at[kind, u],
                device_id={"tile": target}, device_id_type=MESH)

        def halo_ahead_copy(u):
            return halo_copy(block(u), edge_ahead, halo_behind, 0, u, ahead)

        def halo_corner_copy(b):
            return halo_copy(tile(b), edge_ahead, halo_behind, 2, 0, ahead)

        def halo_behind_copy(u):
            return halo_copy(block(u), edge_behind, halo_ahead, 1, u, behind)

        def result_copy(u):
            return pltpu.make_async_remote_copy(
                src_ref=nxt.at[block(u), inner], dst_ref=out_ref.at[block(t), everything],
                send_sem=rsend.at[u], recv_sem=rrecv.at[t],
                device_id={"tile": u}, device_id_type=MESH)

        def result_arrived(u):
            pltpu.make_async_remote_copy(
                src_ref=nxt.at[block(u), inner], dst_ref=out_ref.at[block(u), everything],
                send_sem=rsend.at[u], recv_sem=rrecv.at[u],
                device_id={"tile": behind}, device_id_type=MESH).wait_recv()

        def signal_partner():
            if paired:
                @pl.loop(0, ranks)
                def _(u):
                    @pl.when(u != t)
                    def _():
                        pl.semaphore_signal(go, inc=1, device_id={"tm": partner, "tile": u}, device_id_type=MESH)

        def wait_partner():
            if paired:
                pl.semaphore_wait(go, 1)

        def clear_halo(field, does):
            for missing, place in ((has_behind, halo_behind), (has_ahead, halo_ahead)):
                @pl.when(jnp.logical_not(missing) & does)
                def _(place=place):
                    field[:, place] = jnp.zeros((rows, tr), F32)

        def own_tile(i):
            return tile(t * lt + i)

        def mirror_ahead(field):
            @pl.when(has_ahead)
            def _():
                for i in range(lt):
                    field[own_tile(i), halo_ahead] = field[tile(tile_ahead), pl.ds(tr + i * tr, tr)].T

            @pl.when(has_ahead & has_behind)
            def _():
                field[tile(tile_behind), halo_ahead] = field[tile(tile_ahead), halo_behind].T

        def own_columns(j):
            for i in range(lt // g):
                for c in range(g):
                    for k in range(3):
                        high, low = split(wbuf[j, (t * lt + i * g + c) * 3 + k])
                        at = (j, i, pl.ds((c + k) * tr, tr), pl.ds(c * tr, tr))
                        wc_high[at] = high
                        wc_low[at] = low

        def some_rows(field, j, start, size):
            for i in range(lt // g):
                high, low = split(field[pl.ds(start, size), pl.ds(i * g * tr, span)])
                value = split_dot(high, low, wc_high[j, i], wc_low[j, i])
                at = (j, pl.ds(pl.multiple_of(start + tr, tr), size), pl.ds(i * g * tr, g * tr))
                high, low = split(value)
                m_high[at] = high
                m_low[at] = low

        def group_rows(field, j, u):
            @pl.loop(0, width // chunk)
            def _(r):
                some_rows(field, j, pl.multiple_of(u * width + r * chunk, chunk), chunk)

        def near_rows(field, j):
            @pl.when(has_behind)
            def _():
                some_rows(field, j, pl.multiple_of(tile_behind * tr, tr), tr)
            group_rows(field, j, t)

        def left_rows(j, owner, target, columns, turned):
            @pl.loop(0, lt // g)
            def _(i):
                begin = owner * lt + i * g
                for c in range(g):
                    for k in range(3):
                        high, low = split(wbuf[j, (begin + c) * 3 + k].T)
                        at = (pl.ds(c * tr, tr), pl.ds((c + k) * tr, tr))
                        wt_high[at] = high
                        wt_low[at] = low
                start = pl.multiple_of(begin * tr, tr)
                source = pl.ds(start, span)
                value = split_dot(wt_high[...], wt_low[...], m_high[j, source, :], m_low[j, source, :])
                place = pl.ds(start, g * tr)
                value = loc[j, place, :].astype(F32) + value
                target[place, columns] = value
                if turned:
                    for c in range(g):
                        lanes = pl.ds(pl.multiple_of(tr + (i * g + c) * tr, tr), tr)
                        for q in range(lt):
                            nxt[tile(owner * lt + q), lanes] = value[c * tr:(c + 1) * tr, q * tr:(q + 1) * tr].T

        def diagonal(index, field, offset):
            eye = lax.broadcasted_iota(jnp.int32, (tr, tr), 0) == lax.broadcasted_iota(jnp.int32, (tr, tr), 1)
            for c in range(lt):
                part = field[own_tile(c), pl.ds(offset + c * tr, tr)]
                var_ref[pl.ds(index, 1), pl.ds(c * tr, tr)] = jnp.sum(jnp.where(eye, part, 0.0), axis=0, keepdims=True)

        far_end = t + s * count

        @pl.when(has_behind)
        def _():
            w_copy(1, t).start()
        seeds(lambda copy: copy.start())
        clear_halo(odd, True)
        clear_halo(nxt, has_next)
        pass_on(1)

        @pl.when(has_behind)
        def _():
            w_copy(0, t).start()

        def seeds_here(where, u, kind):
            @pl.when(has_next)
            def _():
                seed_arrived((where, inner), kind, u)
                seed_arrived((where, halo_ahead), kind + 2, u)

            @pl.when(has_next & has_behind)
            def _():
                seed_arrived((where, halo_behind), kind + 1, u)

        def seeds_lead(u):
            seeds_here(lead(u, s), u, 5)

        def seeds_rest(u):
            if lt > 1:
                seeds_here(rest(u, s), u, 0)

        def odd_rows(u):
            @pl.when(u != t)
            def _():
                arrive(1, u)
            left_rows(1, u, odd, inner, False)

            @pl.when(has_behind)
            def _():
                halo_behind_copy(u).start()

            @pl.when(has_ahead & (u == t))
            def _():
                halo_corner_copy(tile_corner).start()

            @pl.when(u != t)
            def _():
                halo_ahead_copy(u).start()

        def near_first():
            @pl.when(has_behind)
            def _():
                halo_corner_copy(tile_behind).wait_recv()
                halo_ahead_copy(t).wait_recv()
                for i in range(lt):
                    odd[tile(tile_behind), pl.ds(tr + i * tr, tr)] = odd[own_tile(i), halo_behind].T
            mirror_ahead(odd)
            near_rows(odd, 0)

        def first_step(u):
            halo_behind_copy(u).wait_recv()

            @pl.when(has_behind)
            def _():
                halo_ahead_copy(u).wait_recv()

            @pl.when(u == ahead)
            def _():
                near_first()
            group_rows(odd, 0, u)

            @pl.when(u == ahead)
            def _():
                left_rows(0, t, out_ref, everything, False)

            @pl.when(u != ahead)
            def _():
                arrive(0, u - s)
                left_rows(0, u - s, out_ref, everything, True)
                result_copy(u - s).start()

        def odd_step(u):
            @pl.when(u != ahead)
            def _():
                seeds_lead(u)
            some_rows(nxt, 1, pl.multiple_of(lead(u, s).start, tr), tr)
            odd_rows(u - s)
            if s < 0:
                @pl.when(has_behind)
                def _():
                    pass_one(0, u)

                @pl.when(u != ahead)
                def _():
                    first_step(u - s)
            seeds_rest(u)
            if lt > 1:
                some_rows(nxt, 1, pl.multiple_of(rest(u, s).start, tr), width - tr)

        @pl.when(has_next)
        def _():
            seed_arrived((block(t), inner), 0, t)

        @pl.when(has_next & has_behind)
        def _():
            seed_arrived((tile(tile_behind), inner), 3, 0)
            seed_arrived((tile(tile_behind), halo_behind), 4, 0)

        @pl.when(has_ahead)
        def _():
            seeds_lead(ahead)

        @pl.when(has_behind)
        def _():
            for i in range(lt):
                nxt[own_tile(i), halo_behind] = nxt[tile(tile_behind), pl.ds(tr + i * tr, tr)].T
        mirror_ahead(nxt)
        own_columns(1)
        own_columns(0)
        near_rows(nxt, 1)
        locals_in.wait()
        groups(t, 1, has_ahead, odd_step)
        odd_rows(far_end)
        diagonal(1, odd, tr)
        if s > 0:
            pass_on(0)
            groups(t, 1, has_ahead, first_step)

        @pl.when(has_ahead)
        def _():
            if s < 0:
                first_step(far_end)
            arrive(0, far_end)

            @pl.when(jnp.logical_not(has_behind))
            def _():
                signal_partner()
            left_rows(0, far_end, out_ref, everything, True)
            wait_partner()
            result_copy(far_end).start()

        @pl.when(jnp.logical_not(has_ahead))
        def _():
            near_first()
            left_rows(0, t, out_ref, everything, False)
        diagonal(0, out_ref, 0)

        @pl.when(has_behind)
        def _():
            @pl.loop(1, ranks - count)
            def _(k):
                result_arrived(t - s * k)

        for j in (1, 0):
            groups(t, 0, has_behind, lambda u, j=j: w_copy(j, u).wait_send())
        seeds(lambda copy: copy.wait_send())
        groups(t, 0, has_behind, lambda u: halo_behind_copy(u).wait_send())

        @pl.when(has_ahead)
        def _():
            halo_corner_copy(tile_corner).wait_send()
        groups(t, 1, has_ahead, lambda u: halo_ahead_copy(u).wait_send())
        groups(t, 1, True, lambda u: result_copy(u).wait_send())

    for remainder, s in ((0, 1), (1, -1)):
        @pl.when(lax.rem(p, 2) == remainder)
        def _(s=s):
            triangle(s)


def per_device(parts, ranks, local_inv, seed_inv, band, pattern):
    rows, width = seed_inv.shape[1:]
    lt, tr = band.shape[1], band.shape[3]
    tiles = rows // tr
    g = 2 if lt % 2 == 0 else 1
    span = (g + 2) * tr
    dma = pltpu.SemaphoreType.DMA
    out, var = pl.pallas_call(
        functools.partial(kernel, parts, ranks),
        out_shape=(pltpu.VMEM((rows, width), F32), pltpu.VMEM((2, width), F32)),
        in_specs=[pl.BlockSpec(memory_space=pltpu.HBM)] * 3 + [pl.BlockSpec(memory_space=pltpu.SMEM)],
        out_specs=(pl.BlockSpec(memory_space=pltpu.VMEM), pl.BlockSpec(memory_space=pltpu.VMEM)),
        scratch_shapes=[
            pltpu.VMEM((rows, width + 2 * tr), F32),
            pltpu.VMEM((rows, width + 2 * tr), F32),
            pltpu.VMEM((2, tiles * 3, tr, tr), F32),
            pltpu.VMEM((2, rows + 2 * tr, width), BF16),
            pltpu.VMEM((2, rows + 2 * tr, width), BF16),
            pltpu.VMEM((2, rows, width), BF16),
            pltpu.VMEM((2, lt // g, span, g * tr), BF16),
            pltpu.VMEM((2, lt // g, span, g * tr), BF16),
            pltpu.VMEM((g * tr, span), BF16),
            pltpu.VMEM((g * tr, span), BF16),
            dma((2, ranks)),
            dma((2, ranks)),
            dma((8, ranks)),
            dma((8, ranks)),
            dma((3, ranks)),
            dma((3, ranks)),
            dma((ranks,)),
            dma((ranks,)),
            dma((3,)),
            pltpu.SemaphoreType.REGULAR,
        ],
        compiler_params=pltpu.CompilerParams(
            collective_id=0, has_side_effects=True, vmem_limit_bytes=58 * 1024 * 1024
        ),
    )(local_inv, seed_inv, band.reshape(2, lt * 3, tr, tr), pattern.transpose(2, 0, 1))
    return out[None], var


def solution(mesh):
    placed = (
        P("tm", None, "tile"),
        P("tm", None, "tile"),
        P("tm", "tile", None, None, None),
        P("tm", "tile", None),
    )
    return jax.shard_map(
        functools.partial(per_device, mesh.shape["tm"], mesh.shape["tile"]),
        mesh=mesh,
        in_specs=placed,
        out_specs=(P("tm", None, "tile"), P("tm", "tile")),
        check_vma=False,
    )
```

```python
import functools

import jax
import jax.numpy as jnp
from jax import lax
from jax.experimental import pallas as pl
from jax.experimental.pallas import tpu as pltpu
from jax.sharding import PartitionSpec as P

F32 = jnp.float32
BF16 = jnp.bfloat16
MESH = pl.DeviceIdType.MESH


def split(value):
    high = value.astype(BF16)
    return high, (value - high.astype(F32)).astype(BF16)


def dot(a, b):
    return lax.dot_general(a, b, (((1,), (0,)), ((), ())), preferred_element_type=F32)


def split_dot(a_high, a_low, b_high, b_low):
    return dot(a_high, b_high) + (dot(a_high, b_low) + dot(a_low, b_high))


def kernel(parts, ranks, local_ref, seed_ref, band_ref, pattern_ref, out_ref, var_ref,
           nxt, odd, wbuf, m_high, m_low, loc, wc_high, wc_low, wt_high, wt_low,
           wsend, wrecv, nsend, nrecv, esend, erecv, hsend, hrecv, rsend, rrecv, lsem, go):
    p, t = lax.axis_index("tm"), lax.axis_index("tile")
    rows, width = seed_ref.shape[1], seed_ref.shape[2]
    tr = wbuf.shape[3]
    lt = width // tr
    g = 2 if lt % 2 == 0 else 1
    span = (g + 2) * tr
    chunk = 256 if width % 256 == 0 else tr
    inner = pl.ds(tr, width)
    everything = pl.ds(0, width)
    has_next = p < parts - 1

    barrier = pltpu.get_barrier_semaphore()

    paired = parts % 2 == 0
    partner = p + 1 - 2 * lax.rem(p, 2)

    def greet(q, u):
        pl.semaphore_signal(barrier, inc=1, device_id={"tm": q, "tile": u}, device_id_type=MESH)

    @pl.loop(0, ranks)
    def _(u):
        @pl.when(u != t)
        def _():
            greet(p, u)
        if paired:
            greet(partner, u)

    for a in (-1, 1):
        for b in (-1, 0, 1):
            meet = (p + a >= 0) & (p + a < parts) & (t + b >= 0) & (t + b < ranks)

            @pl.when(meet & (p + a != partner) if paired else meet)
            def _(a=a, b=b):
                greet(p + a, t + b)
    near_tm = jnp.where(p > 0, 1, 0) + jnp.where(p < parts - 1, 1, 0) - (1 if paired else 0)
    near_tile = 1 + jnp.where(t > 0, 1, 0) + jnp.where(t < ranks - 1, 1, 0)
    meets = ranks - 1 + (ranks if paired else 0) + near_tm * near_tile
    own_local = [pltpu.make_async_copy(band_ref.at[j], wbuf.at[j, pl.ds(t * lt * 3, lt * 3)], lsem.at[j]) for j in (0, 1)]
    locals_in = pltpu.make_async_copy(local_ref, loc, lsem.at[2])
    for copy in own_local[::-1]:
        copy.start()
    locals_in.start()

    @pl.when(p == parts - 1)
    def _():
        nxt[...] = jnp.zeros_like(nxt)

    for ref in (m_high, m_low):
        for j in (0, 1):
            ref[j, pl.ds(0, tr), :] = jnp.zeros((tr, width), BF16)
            ref[j, pl.ds(tr + rows, tr), :] = jnp.zeros((tr, width), BF16)
    for ref in (wc_high, wc_low, wt_high, wt_low):
        ref[...] = jnp.zeros_like(ref)
    for j in (1, 0):
        own_local[j].wait()
        for b in range(lt):
            for k in range(3):
                at = (j, (t * lt + b) * 3 + k)
                wbuf[at] = wbuf[at] * pattern_ref[k, j, b].astype(F32)
    pl.semaphore_wait(barrier, meets)

    def block(u):
        return pl.ds(pl.multiple_of(u * width, width), width)

    def tile(b):
        return pl.ds(pl.multiple_of(b * tr, tr), tr)

    def triangle(s):
        behind, ahead = t - s, t + s
        count = ranks - 1 - t if s > 0 else t
        has_behind, has_ahead = (t > 0, t < ranks - 1) if s > 0 else (t < ranks - 1, t > 0)
        first, last = pl.ds(tr, tr), pl.ds(width, tr)
        left, right = pl.ds(0, tr), pl.ds(tr + width, tr)
        edge_behind, edge_ahead = (first, last) if s > 0 else (last, first)
        halo_behind, halo_ahead = (left, right) if s > 0 else (right, left)
        tile_behind, tile_ahead = (t * lt - 1, (t + 1) * lt) if s > 0 else ((t + 1) * lt, t * lt - 1)
        tile_corner = (t + 1) * lt - 1 if s > 0 else t * lt

        def groups(base, start, does, action):
            number = ranks - 1 - base if s > 0 else base

            @pl.when(does)
            def _():
                @pl.loop(start, number + 1)
                def _(k):
                    action(base + s * k)


        def w_copy(j, u):
            part = wbuf.at[j, pl.ds(u * lt * 3, lt * 3)]
            return pltpu.make_async_remote_copy(
                src_ref=part, dst_ref=part, send_sem=wsend.at[j, u], recv_sem=wrecv.at[j, u],
                device_id={"tile": behind}, device_id_type=MESH)

        def pass_one(j, u):
            w_copy(j, u).wait_recv()
            w_copy(j, u).start()

        def pass_on(j):
            groups(t, 1, has_behind, lambda u: pass_one(j, u))

        def arrive(j, u):
            @pl.when(jnp.logical_not(has_behind))
            def _():
                w_copy(j, u).wait_recv()


        def seed_copy(src, dst, kind, u, target):
            return pltpu.make_async_remote_copy(
                src_ref=seed_ref.at[(0,) + src], dst_ref=nxt.at[dst],
                send_sem=nsend.at[kind, u], recv_sem=nrecv.at[kind, u],
                device_id={"tm": p - 1, "tile": target}, device_id_type=MESH)

        def lead(u, direction):
            return tile(u * lt if direction > 0 else (u + 1) * lt - 1)

        def rest(u, direction):
            return pl.ds(pl.multiple_of(u * width + (tr if direction > 0 else 0), tr), width - tr)

        def seeds(action):
            low, high = pl.ds(0, tr), pl.ds(width - tr, tr)
            toward, back = (low, high) if s > 0 else (high, low)
            number = t if s > 0 else ranks - 1 - t

            def pieces(u, source, place, kind, target):
                action(seed_copy((lead(u, -s), source), (lead(u, -s), place), kind + 1, u, target))
                if lt > 1:
                    action(seed_copy((rest(u, -s), source), (rest(u, -s), place), kind, u, target))

            @pl.when(p > 0)
            def _():
                @pl.when(has_ahead)
                def _():
                    row = tile(tile_ahead)
                    action(seed_copy((row, everything), (row, inner), 6, 0, t))

                if s < 0:
                    @pl.when(has_behind)
                    def _():
                        corner = tile((t + 1) * lt - 1)
                        action(seed_copy((corner, toward), (corner, halo_ahead), 7, 0, behind))
                action(seed_copy((block(t), everything), (block(t), inner), 0, t, t))

                if s < 0:
                    @pl.when(has_ahead)
                    def _():
                        pieces(t, back, halo_behind, 4, ahead)

                @pl.loop(1, number + 1)
                def _(k):
                    u = t - s * k
                    pieces(u, everything, inner, 0, t)
                    if s < 0:
                        @pl.when(has_ahead)
                        def _():
                            pieces(u, back, halo_behind, 4, ahead)

                        @pl.when(k > 1)
                        def _():
                            pieces(u, toward, halo_ahead, 2, behind)

        def seed_arrived(place, lanes, kind, u):
            pltpu.make_async_remote_copy(
                src_ref=nxt.at[place, lanes], dst_ref=nxt.at[place, lanes],
                send_sem=nsend.at[kind, u], recv_sem=nrecv.at[kind, u],
                device_id={"tile": behind}, device_id_type=MESH).wait_recv()

        def edge_copy(place, source, target_place, kind, u, target):
            return pltpu.make_async_remote_copy(
                src_ref=nxt.at[place, source], dst_ref=nxt.at[place, target_place],
                send_sem=esend.at[kind, u], recv_sem=erecv.at[kind, u],
                device_id={"tile": target}, device_id_type=MESH)

        def edge_ahead_copy(place, kind, u):
            return edge_copy(place, edge_ahead, halo_behind, kind, u, ahead)

        def edge_behind_copy(place, kind, u):
            return edge_copy(place, edge_behind, halo_ahead, kind + 2, u, behind)

        def edges(place, kind, u, action):
            @pl.when(has_behind)
            def _():
                action(edge_behind_copy(place, kind, u))

            @pl.when((u != t) & (u != ahead))
            def _():
                action(edge_ahead_copy(place, kind, u))

        def all_edges(action):
            @pl.when(has_next)
            def _():
                @pl.loop(0, count + 1)
                def _(k):
                    group_edges(t + s * k, action)

                @pl.when(has_ahead)
                def _():
                    action(edge_ahead_copy(tile(tile_corner), 4, 0))

        def group_edges(u, action):
            edges(lead(u, s), 1, u, action)
            if lt > 1:
                edges(rest(u, s), 0, u, action)

        def halo_copy(place, source, target_place, kind, u, target):
            return pltpu.make_async_remote_copy(
                src_ref=odd.at[place, source], dst_ref=odd.at[place, target_place],
                send_sem=hsend.at[kind, u], recv_sem=hrecv.at[kind, u],
                device_id={"tile": target}, device_id_type=MESH)

        def halo_ahead_copy(u):
            return halo_copy(block(u), edge_ahead, halo_behind, 0, u, ahead)

        def halo_corner_copy(b):
            return halo_copy(tile(b), edge_ahead, halo_behind, 2, 0, ahead)

        def halo_behind_copy(u):
            return halo_copy(block(u), edge_behind, halo_ahead, 1, u, behind)

        def result_copy(u):
            return pltpu.make_async_remote_copy(
                src_ref=nxt.at[block(u), inner], dst_ref=out_ref.at[block(t), everything],
                send_sem=rsend.at[u], recv_sem=rrecv.at[t],
                device_id={"tile": u}, device_id_type=MESH)

        def result_arrived(u):
            pltpu.make_async_remote_copy(
                src_ref=nxt.at[block(u), inner], dst_ref=out_ref.at[block(u), everything],
                send_sem=rsend.at[u], recv_sem=rrecv.at[u],
                device_id={"tile": behind}, device_id_type=MESH).wait_recv()

        def signal_partner():
            if paired:
                @pl.loop(0, ranks)
                def _(u):
                    @pl.when(u != t)
                    def _():
                        pl.semaphore_signal(go, inc=1, device_id={"tm": partner, "tile": u}, device_id_type=MESH)

        def wait_partner():
            if paired:
                pl.semaphore_wait(go, 1)

        def clear_halo(field, does):
            for missing, place in ((has_behind, halo_behind), (has_ahead, halo_ahead)):
                @pl.when(jnp.logical_not(missing) & does)
                def _(place=place):
                    field[:, place] = jnp.zeros((rows, tr), F32)

        def own_tile(i):
            return tile(t * lt + i)

        def mirror_ahead(field):
            @pl.when(has_ahead)
            def _():
                for i in range(lt):
                    field[own_tile(i), halo_ahead] = field[tile(tile_ahead), pl.ds(tr + i * tr, tr)].T

            @pl.when(has_ahead & has_behind)
            def _():
                field[tile(tile_behind), halo_ahead] = field[tile(tile_ahead), halo_behind].T

        def own_columns(j):
            for i in range(lt // g):
                for c in range(g):
                    for k in range(3):
                        high, low = split(wbuf[j, (t * lt + i * g + c) * 3 + k])
                        at = (j, i, pl.ds((c + k) * tr, tr), pl.ds(c * tr, tr))
                        wc_high[at] = high
                        wc_low[at] = low

        def some_rows(field, j, start, size):
            for i in range(lt // g):
                high, low = split(field[pl.ds(start, size), pl.ds(i * g * tr, span)])
                value = split_dot(high, low, wc_high[j, i], wc_low[j, i])
                at = (j, pl.ds(pl.multiple_of(start + tr, tr), size), pl.ds(i * g * tr, g * tr))
                high, low = split(value)
                m_high[at] = high
                m_low[at] = low

        def group_rows(field, j, u):
            @pl.loop(0, width // chunk)
            def _(r):
                some_rows(field, j, pl.multiple_of(u * width + r * chunk, chunk), chunk)

        def near_rows(field, j):
            @pl.when(has_behind)
            def _():
                some_rows(field, j, pl.multiple_of(tile_behind * tr, tr), tr)
            group_rows(field, j, t)

        def left_rows(j, owner, target, columns, turned):
            @pl.loop(0, lt // g)
            def _(i):
                begin = owner * lt + i * g
                for c in range(g):
                    for k in range(3):
                        high, low = split(wbuf[j, (begin + c) * 3 + k].T)
                        at = (pl.ds(c * tr, tr), pl.ds((c + k) * tr, tr))
                        wt_high[at] = high
                        wt_low[at] = low
                start = pl.multiple_of(begin * tr, tr)
                source = pl.ds(start, span)
                value = split_dot(wt_high[...], wt_low[...], m_high[j, source, :], m_low[j, source, :])
                place = pl.ds(start, g * tr)
                value = loc[j, place, :].astype(F32) + value
                target[place, columns] = value
                if turned:
                    for c in range(g):
                        lanes = pl.ds(pl.multiple_of(tr + (i * g + c) * tr, tr), tr)
                        for q in range(lt):
                            nxt[tile(owner * lt + q), lanes] = value[c * tr:(c + 1) * tr, q * tr:(q + 1) * tr].T

        def diagonal(index, field, offset):
            eye = lax.broadcasted_iota(jnp.int32, (tr, tr), 0) == lax.broadcasted_iota(jnp.int32, (tr, tr), 1)
            for c in range(lt):
                part = field[own_tile(c), pl.ds(offset + c * tr, tr)]
                var_ref[pl.ds(index, 1), pl.ds(c * tr, tr)] = jnp.sum(jnp.where(eye, part, 0.0), axis=0, keepdims=True)

        far_end = t + s * count

        @pl.when(has_behind)
        def _():
            w_copy(1, t).start()
        seeds(lambda copy: copy.start())
        clear_halo(odd, True)
        clear_halo(nxt, has_next)
        own_columns(1)
        own_columns(0)

        def near_seeds():
            @pl.when(has_next)
            def _():
                seed_arrived(block(t), inner, 0, t)
                if s < 0:
                    group_edges(t, lambda copy: copy.start())

                    @pl.when(has_ahead)
                    def _():
                        edge_ahead_copy(tile(tile_corner), 4, 0).start()

        def column_seeds(u):
            @pl.when(has_next)
            def _():
                seed_arrived(lead(u, s), inner, 1, u)
                if lt > 1:
                    seed_arrived(rest(u, s), inner, 0, u)
                group_edges(u, lambda copy: copy.start())

        def seeds_here(place, kind, u):
            if s > 0:
                @pl.when(has_next)
                def _():
                    seed_arrived(place, inner, kind, u)
                    seed_arrived(place, halo_ahead, kind + 4, u)

                @pl.when(has_next & has_behind)
                def _():
                    seed_arrived(place, halo_behind, kind + 2, u)
            else:
                @pl.when(has_next)
                def _():
                    edge_behind_copy(place, kind, u).wait_recv()

                @pl.when(has_next & has_behind)
                def _():
                    edge_ahead_copy(place, kind, u).wait_recv()

        def seeds_lead(u):
            seeds_here(lead(u, s), 1, u)

        def seeds_rest(u):
            if lt > 1:
                seeds_here(rest(u, s), 0, u)

        def near_odd():
            @pl.when(has_next & has_behind)
            def _():
                seed_arrived(tile(tile_behind), inner, 6, 0)
                if s > 0:
                    seed_arrived(tile(tile_behind), halo_behind, 7, 0)
                else:
                    edge_ahead_copy(tile(tile_behind), 4, 0).wait_recv()

            @pl.when(has_behind)
            def _():
                for i in range(lt):
                    nxt[own_tile(i), halo_behind] = nxt[tile(tile_behind), pl.ds(tr + i * tr, tr)].T
            mirror_ahead(nxt)
            near_rows(nxt, 1)

        def odd_rows(u):
            @pl.when(u != t)
            def _():
                arrive(1, u)
            left_rows(1, u, odd, inner, False)

            @pl.when(has_behind)
            def _():
                halo_behind_copy(u).start()

            @pl.when(has_ahead & (u == t))
            def _():
                halo_corner_copy(tile_corner).start()

            @pl.when(u != t)
            def _():
                halo_ahead_copy(u).start()

        def near_first():
            @pl.when(has_behind)
            def _():
                halo_corner_copy(tile_behind).wait_recv()
                halo_ahead_copy(t).wait_recv()
                for i in range(lt):
                    odd[tile(tile_behind), pl.ds(tr + i * tr, tr)] = odd[own_tile(i), halo_behind].T
            mirror_ahead(odd)
            near_rows(odd, 0)

        def first_step(u):
            halo_behind_copy(u).wait_recv()

            @pl.when(has_behind)
            def _():
                halo_ahead_copy(u).wait_recv()

            @pl.when(u == ahead)
            def _():
                near_first()
            group_rows(odd, 0, u)

            @pl.when(u == ahead)
            def _():
                left_rows(0, t, out_ref, everything, False)

            @pl.when(u != ahead)
            def _():
                arrive(0, u - s)
                left_rows(0, u - s, out_ref, everything, True)
                result_copy(u - s).start()

        def odd_step(u):
            seeds_lead(u)

            @pl.when(u == ahead)
            def _():
                near_odd()
            some_rows(nxt, 1, pl.multiple_of(lead(u, s).start, tr), tr)
            odd_rows(u - s)
            seeds_rest(u)
            if lt > 1:
                some_rows(nxt, 1, pl.multiple_of(rest(u, s).start, tr), width - tr)

        locals_in.wait()
        if s > 0:
            pass_on(1)

            @pl.when(has_behind)
            def _():
                w_copy(0, t).start()
            near_seeds()
            groups(t, 1, has_ahead, odd_step)
        else:
            @pl.when(has_behind & has_ahead)
            def _():
                pass_one(1, ahead)
            near_seeds()

            @pl.when(has_behind)
            def _():
                w_copy(0, t).start()

            def seed_step(u):
                @pl.when(has_behind & (u != ahead))
                def _():
                    pass_one(1, u)
                column_seeds(u)

                @pl.when(jnp.logical_not(has_behind))
                def _():
                    odd_step(u)
            groups(t, 1, has_ahead, seed_step)

            def odd_later(u):
                @pl.when((u != far_end) | (count != ranks - 2))
                def _():
                    pass_one(0, u)
            groups(t, 1, has_behind & has_ahead, odd_later)
            groups(t, 1, has_behind & has_ahead, odd_step)

        @pl.when(jnp.logical_not(has_ahead))
        def _():
            near_odd()
        odd_rows(far_end)
        diagonal(1, odd, tr)
        if s > 0:
            pass_on(0)
        else:
            @pl.when(has_ahead & (count == ranks - 2))
            def _():
                pass_one(0, far_end)
            all_edges(lambda copy: copy.wait_send())
        groups(t, 1, has_ahead, first_step)

        @pl.when(has_ahead)
        def _():
            arrive(0, far_end)

            @pl.when(jnp.logical_not(has_behind))
            def _():
                signal_partner()
            left_rows(0, far_end, out_ref, everything, True)
            wait_partner()
            result_copy(far_end).start()

        @pl.when(jnp.logical_not(has_ahead))
        def _():
            near_first()
            left_rows(0, t, out_ref, everything, False)
        diagonal(0, out_ref, 0)

        @pl.when(has_behind)
        def _():
            @pl.loop(1, ranks - count)
            def _(k):
                result_arrived(t - s * k)

        for j in (1, 0):
            groups(t, 0, has_behind, lambda u, j=j: w_copy(j, u).wait_send())
        seeds(lambda copy: copy.wait_send())
        groups(t, 0, has_behind, lambda u: halo_behind_copy(u).wait_send())

        @pl.when(has_ahead)
        def _():
            halo_corner_copy(tile_corner).wait_send()
        groups(t, 1, has_ahead, lambda u: halo_ahead_copy(u).wait_send())
        groups(t, 1, True, lambda u: result_copy(u).wait_send())

    for remainder, s in ((0, 1), (1, -1)):
        @pl.when(lax.rem(p, 2) == remainder)
        def _(s=s):
            triangle(s)


def per_device(parts, ranks, local_inv, seed_inv, band, pattern):
    rows, width = seed_inv.shape[1:]
    lt, tr = band.shape[1], band.shape[3]
    tiles = rows // tr
    g = 2 if lt % 2 == 0 else 1
    span = (g + 2) * tr
    dma = pltpu.SemaphoreType.DMA
    out, var = pl.pallas_call(
        functools.partial(kernel, parts, ranks),
        out_shape=(pltpu.VMEM((rows, width), F32), pltpu.VMEM((2, width), F32)),
        in_specs=[pl.BlockSpec(memory_space=pltpu.HBM)] * 3 + [pl.BlockSpec(memory_space=pltpu.SMEM)],
        out_specs=(pl.BlockSpec(memory_space=pltpu.VMEM), pl.BlockSpec(memory_space=pltpu.VMEM)),
        scratch_shapes=[
            pltpu.VMEM((rows, width + 2 * tr), F32),
            pltpu.VMEM((rows, width + 2 * tr), F32),
            pltpu.VMEM((2, tiles * 3, tr, tr), F32),
            pltpu.VMEM((2, rows + 2 * tr, width), BF16),
            pltpu.VMEM((2, rows + 2 * tr, width), BF16),
            pltpu.VMEM((2, rows, width), BF16),
            pltpu.VMEM((2, lt // g, span, g * tr), BF16),
            pltpu.VMEM((2, lt // g, span, g * tr), BF16),
            pltpu.VMEM((g * tr, span), BF16),
            pltpu.VMEM((g * tr, span), BF16),
            dma((2, ranks)),
            dma((2, ranks)),
            dma((8, ranks)),
            dma((8, ranks)),
            dma((5, ranks)),
            dma((5, ranks)),
            dma((3, ranks)),
            dma((3, ranks)),
            dma((ranks,)),
            dma((ranks,)),
            dma((3,)),
            pltpu.SemaphoreType.REGULAR,
        ],
        compiler_params=pltpu.CompilerParams(
            collective_id=0, has_side_effects=True, vmem_limit_bytes=58 * 1024 * 1024
        ),
    )(local_inv, seed_inv, band.reshape(2, lt * 3, tr, tr), pattern.transpose(2, 0, 1))
    return out[None], var


def solution(mesh):
    placed = (
        P("tm", None, "tile"),
        P("tm", None, "tile"),
        P("tm", "tile", None, None, None),
        P("tm", "tile", None),
    )
    return jax.shard_map(
        functools.partial(per_device, mesh.shape["tm"], mesh.shape["tile"]),
        mesh=mesh,
        in_specs=placed,
        out_specs=(P("tm", None, "tile"), P("tm", "tile")),
        check_vma=False,
    )
```

```python
import functools

import jax
import jax.numpy as jnp
from jax import lax
from jax.experimental import pallas as pl
from jax.experimental.pallas import tpu as pltpu
from jax.sharding import PartitionSpec as P

F32 = jnp.float32
BF16 = jnp.bfloat16
MESH = pl.DeviceIdType.MESH


def split(value):
    high = value.astype(BF16)
    return high, (value - high.astype(F32)).astype(BF16)


def dot(a, b):
    return lax.dot_general(a, b, (((1,), (0,)), ((), ())), preferred_element_type=F32)


def split_dot(a_high, a_low, b_high, b_low):
    return dot(a_high, b_high) + (dot(a_high, b_low) + dot(a_low, b_high))


def kernel(parts, ranks, local_ref, seed_ref, band_ref, pattern_ref, out_ref, var_ref,
           nxt, odd, wbuf, m_high, m_low, loc, wc_high, wc_low, wt_high, wt_low,
           wsend, wrecv, nsend, nrecv, esend, erecv, hsend, hrecv, rsend, rrecv, lsem, go):
    p, t = lax.axis_index("tm"), lax.axis_index("tile")
    rows, width = seed_ref.shape[1], seed_ref.shape[2]
    tr = wbuf.shape[3]
    lt = width // tr
    g = 2 if lt % 2 == 0 else 1
    span = (g + 2) * tr
    chunk = 256 if width % 256 == 0 else tr
    inner = pl.ds(tr, width)
    everything = pl.ds(0, width)
    has_next = p < parts - 1

    barrier = pltpu.get_barrier_semaphore()

    paired = parts % 2 == 0
    partner = p + 1 - 2 * lax.rem(p, 2)

    def greet(q, u):
        pl.semaphore_signal(barrier, inc=1, device_id={"tm": q, "tile": u}, device_id_type=MESH)

    @pl.loop(0, ranks)
    def _(u):
        @pl.when(u != t)
        def _():
            greet(p, u)
        if paired:
            greet(partner, u)

    for a in (-1, 1):
        for b in (-1, 0, 1):
            meet = (p + a >= 0) & (p + a < parts) & (t + b >= 0) & (t + b < ranks)

            @pl.when(meet & (p + a != partner) if paired else meet)
            def _(a=a, b=b):
                greet(p + a, t + b)
    near_tm = jnp.where(p > 0, 1, 0) + jnp.where(p < parts - 1, 1, 0) - (1 if paired else 0)
    near_tile = 1 + jnp.where(t > 0, 1, 0) + jnp.where(t < ranks - 1, 1, 0)
    meets = ranks - 1 + (ranks if paired else 0) + near_tm * near_tile
    own_local = [pltpu.make_async_copy(band_ref.at[j], wbuf.at[j, pl.ds(t * lt * 3, lt * 3)], lsem.at[j]) for j in (0, 1)]
    locals_in = pltpu.make_async_copy(local_ref, loc, lsem.at[2])
    for copy in own_local[::-1]:
        copy.start()
    locals_in.start()

    @pl.when(p == parts - 1)
    def _():
        nxt[...] = jnp.zeros_like(nxt)

    for ref in (m_high, m_low):
        for j in (0, 1):
            ref[j, pl.ds(0, tr), :] = jnp.zeros((tr, width), BF16)
            ref[j, pl.ds(tr + rows, tr), :] = jnp.zeros((tr, width), BF16)
    for ref in (wc_high, wc_low, wt_high, wt_low):
        ref[...] = jnp.zeros_like(ref)
    for j in (0, 1):
        @pl.when(t > 0)
        def _(j=j):
            wbuf[j, 0] = jnp.zeros((tr, tr), F32)

        @pl.when(t < ranks - 1)
        def _(j=j):
            wbuf[j, wbuf.shape[1] - 1] = jnp.zeros((tr, tr), F32)
    for j in (1, 0):
        own_local[j].wait()
        for b in range(lt):
            for k in range(3):
                at = (j, (t * lt + b) * 3 + k)
                wbuf[at] = wbuf[at] * pattern_ref[k, j, b].astype(F32)
    pl.semaphore_wait(barrier, meets)

    def block(u):
        return pl.ds(pl.multiple_of(u * width, width), width)

    def tile(b):
        return pl.ds(pl.multiple_of(b * tr, tr), tr)

    def triangle(s):
        behind, ahead = t - s, t + s
        count = ranks - 1 - t if s > 0 else t
        has_behind, has_ahead = (t > 0, t < ranks - 1) if s > 0 else (t < ranks - 1, t > 0)
        first, last = pl.ds(tr, tr), pl.ds(width, tr)
        left, right = pl.ds(0, tr), pl.ds(tr + width, tr)
        edge_behind, edge_ahead = (first, last) if s > 0 else (last, first)
        halo_behind, halo_ahead = (left, right) if s > 0 else (right, left)
        tile_behind, tile_ahead = (t * lt - 1, (t + 1) * lt) if s > 0 else ((t + 1) * lt, t * lt - 1)
        end = ranks - 1 if s > 0 else 0
        tile_corner = (t + 1) * lt - 1 if s > 0 else t * lt

        def groups(base, start, does, action):
            number = ranks - 1 - base if s > 0 else base

            @pl.when(does)
            def _():
                @pl.loop(start, number + 1)
                def _(k):
                    action(base + s * k)


        def w_copy(j, u, action):
            for condition, skip in ((u == end, 1), (u != end, 0)):
                @pl.when(condition)
                def _(skip=skip):
                    part = wbuf.at[j, pl.ds(u * lt * 3 + (skip if s < 0 else 0), lt * 3 - skip)]
                    action(pltpu.make_async_remote_copy(
                        src_ref=part, dst_ref=part, send_sem=wsend.at[j, u], recv_sem=wrecv.at[j, u],
                        device_id={"tile": behind}, device_id_type=MESH))

        def w_start(j, u):
            w_copy(j, u, lambda copy: copy.start())

        def w_here(j, u):
            w_copy(j, u, lambda copy: copy.wait_recv())

        def pass_one(j, u):
            w_here(j, u)
            w_start(j, u)

        def pass_on(j):
            groups(t, 1, has_behind, lambda u: pass_one(j, u))

        def arrive(j, u):
            @pl.when(jnp.logical_not(has_behind))
            def _():
                w_here(j, u)


        def seed_copy(src, dst, kind, u, target):
            return pltpu.make_async_remote_copy(
                src_ref=seed_ref.at[(0,) + src], dst_ref=nxt.at[dst],
                send_sem=nsend.at[kind, u], recv_sem=nrecv.at[kind, u],
                device_id={"tm": p - 1, "tile": target}, device_id_type=MESH)

        def own_strip(c):
            return pl.ds(pl.multiple_of(t * width + c * tr, tr), width - c * tr)

        def lead(u, direction):
            return tile(u * lt if direction > 0 else (u + 1) * lt - 1)

        def rest(u, direction):
            return pl.ds(pl.multiple_of(u * width + (tr if direction > 0 else 0), tr), width - tr)

        def seeds(action):
            low, high = pl.ds(0, tr), pl.ds(width - tr, tr)
            toward, back = (low, high) if s > 0 else (high, low)
            number = t if s > 0 else ranks - 1 - t

            def pieces(u, source, place, kind, target):
                action(seed_copy((lead(u, -s), source), (lead(u, -s), place), kind + 1, u, target))
                if lt > 1:
                    action(seed_copy((rest(u, -s), source), (rest(u, -s), place), kind, u, target))

            @pl.when(p > 0)
            def _():
                @pl.when(has_ahead)
                def _():
                    row = tile(tile_ahead)
                    action(seed_copy((row, everything), (row, inner), 6, 0, t))

                if s < 0:
                    @pl.when(has_behind)
                    def _():
                        corner = tile((t + 1) * lt - 1)
                        action(seed_copy((corner, toward), (corner, halo_ahead), 7, 0, behind))
                for c in range(lt):
                    strip = own_strip(c)
                    action(seed_copy((strip, pl.ds(c * tr, tr)), (strip, pl.ds(tr + c * tr, tr)), 8, c, t))

                if s < 0:
                    @pl.when(has_ahead)
                    def _():
                        pieces(t, back, halo_behind, 4, ahead)

                @pl.loop(1, number + 1)
                def _(k):
                    u = t - s * k
                    pieces(u, everything, inner, 0, t)
                    if s < 0:
                        @pl.when(has_ahead)
                        def _():
                            pieces(u, back, halo_behind, 4, ahead)

                        @pl.when(k > 1)
                        def _():
                            pieces(u, toward, halo_ahead, 2, behind)

        def seed_arrived(place, lanes, kind, u):
            pltpu.make_async_remote_copy(
                src_ref=nxt.at[place, lanes], dst_ref=nxt.at[place, lanes],
                send_sem=nsend.at[kind, u], recv_sem=nrecv.at[kind, u],
                device_id={"tile": behind}, device_id_type=MESH).wait_recv()

        def edge_copy(place, source, target_place, kind, u, target):
            return pltpu.make_async_remote_copy(
                src_ref=nxt.at[place, source], dst_ref=nxt.at[place, target_place],
                send_sem=esend.at[kind, u], recv_sem=erecv.at[kind, u],
                device_id={"tile": target}, device_id_type=MESH)

        def edge_ahead_copy(place, kind, u):
            return edge_copy(place, edge_ahead, halo_behind, kind, u, ahead)

        def edge_behind_copy(place, kind, u):
            return edge_copy(place, edge_behind, halo_ahead, kind + 2, u, behind)

        def edges(place, kind, u, action):
            @pl.when(has_behind)
            def _():
                action(edge_behind_copy(place, kind, u))

            @pl.when((u != t) & (u != ahead))
            def _():
                action(edge_ahead_copy(place, kind, u))

        def all_edges(action):
            @pl.when(has_next)
            def _():
                @pl.loop(0, count + 1)
                def _(k):
                    group_edges(t + s * k, action)

                @pl.when(has_ahead)
                def _():
                    action(edge_ahead_copy(tile(tile_corner), 4, 0))

        def group_edges(u, action):
            edges(lead(u, s), 1, u, action)
            if lt > 1:
                edges(rest(u, s), 0, u, action)

        def halo_copy(place, source, target_place, kind, u, target):
            return pltpu.make_async_remote_copy(
                src_ref=odd.at[place, source], dst_ref=odd.at[place, target_place],
                send_sem=hsend.at[kind, u], recv_sem=hrecv.at[kind, u],
                device_id={"tile": target}, device_id_type=MESH)

        def halo_ahead_copy(u):
            return halo_copy(block(u), edge_ahead, halo_behind, 0, u, ahead)

        def halo_corner_copy(b):
            return halo_copy(tile(b), edge_ahead, halo_behind, 2, 0, ahead)

        def halo_behind_copy(u):
            return halo_copy(block(u), edge_behind, halo_ahead, 1, u, behind)

        def result_copy(u):
            return pltpu.make_async_remote_copy(
                src_ref=nxt.at[block(u), inner], dst_ref=out_ref.at[block(t), everything],
                send_sem=rsend.at[u], recv_sem=rrecv.at[t],
                device_id={"tile": u}, device_id_type=MESH)

        def result_arrived(u):
            pltpu.make_async_remote_copy(
                src_ref=nxt.at[block(u), inner], dst_ref=out_ref.at[block(u), everything],
                send_sem=rsend.at[u], recv_sem=rrecv.at[u],
                device_id={"tile": behind}, device_id_type=MESH).wait_recv()

        def signal_partner():
            if paired:
                @pl.loop(0, ranks)
                def _(u):
                    @pl.when(u != t)
                    def _():
                        pl.semaphore_signal(go, inc=1, device_id={"tm": partner, "tile": u}, device_id_type=MESH)

        def wait_partner():
            if paired:
                pl.semaphore_wait(go, 1)

        def clear_halo(field, does):
            for missing, place in ((has_behind, halo_behind), (has_ahead, halo_ahead)):
                @pl.when(jnp.logical_not(missing) & does)
                def _(place=place):
                    field[:, place] = jnp.zeros((rows, tr), F32)

        def own_tile(i):
            return tile(t * lt + i)

        def mirror_ahead(field):
            @pl.when(has_ahead)
            def _():
                for i in range(lt):
                    field[own_tile(i), halo_ahead] = field[tile(tile_ahead), pl.ds(tr + i * tr, tr)].T

            @pl.when(has_ahead & has_behind)
            def _():
                field[tile(tile_behind), halo_ahead] = field[tile(tile_ahead), halo_behind].T

        def own_columns(j):
            for i in range(lt // g):
                for c in range(g):
                    for k in range(3):
                        high, low = split(wbuf[j, (t * lt + i * g + c) * 3 + k])
                        at = (j, i, pl.ds((c + k) * tr, tr), pl.ds(c * tr, tr))
                        wc_high[at] = high
                        wc_low[at] = low

        def some_rows(field, j, start, size):
            for i in range(lt // g):
                high, low = split(field[pl.ds(start, size), pl.ds(i * g * tr, span)])
                value = split_dot(high, low, wc_high[j, i], wc_low[j, i])
                at = (j, pl.ds(pl.multiple_of(start + tr, tr), size), pl.ds(i * g * tr, g * tr))
                high, low = split(value)
                m_high[at] = high
                m_low[at] = low

        def group_rows(field, j, u):
            @pl.loop(0, width // chunk)
            def _(r):
                some_rows(field, j, pl.multiple_of(u * width + r * chunk, chunk), chunk)

        def near_rows(field, j):
            @pl.when(has_behind)
            def _():
                some_rows(field, j, pl.multiple_of(tile_behind * tr, tr), tr)
            group_rows(field, j, t)

        def left_rows(j, owner, target, columns, turned):
            @pl.loop(0, lt // g)
            def _(i):
                begin = owner * lt + i * g
                for c in range(g):
                    for k in range(3):
                        high, low = split(wbuf[j, (begin + c) * 3 + k].T)
                        at = (pl.ds(c * tr, tr), pl.ds((c + k) * tr, tr))
                        wt_high[at] = high
                        wt_low[at] = low
                start = pl.multiple_of(begin * tr, tr)
                source = pl.ds(start, span)
                value = split_dot(wt_high[...], wt_low[...], m_high[j, source, :], m_low[j, source, :])
                place = pl.ds(start, g * tr)
                value = loc[j, place, :].astype(F32) + value
                target[place, columns] = value
                if turned:
                    for c in range(g):
                        lanes = pl.ds(pl.multiple_of(tr + (i * g + c) * tr, tr), tr)
                        for q in range(lt):
                            nxt[tile(owner * lt + q), lanes] = value[c * tr:(c + 1) * tr, q * tr:(q + 1) * tr].T

        def diagonal(index, field, offset):
            eye = lax.broadcasted_iota(jnp.int32, (tr, tr), 0) == lax.broadcasted_iota(jnp.int32, (tr, tr), 1)
            for c in range(lt):
                part = field[own_tile(c), pl.ds(offset + c * tr, tr)]
                var_ref[pl.ds(index, 1), pl.ds(c * tr, tr)] = jnp.sum(jnp.where(eye, part, 0.0), axis=0, keepdims=True)

        far_end = t + s * count

        @pl.when(has_behind)
        def _():
            w_start(1, t)
        seeds(lambda copy: copy.start())
        clear_halo(odd, True)
        clear_halo(nxt, has_next)
        own_columns(1)
        own_columns(0)

        def near_seeds():
            @pl.when(has_next)
            def _():
                for c in range(lt):
                    seed_arrived(own_strip(c), pl.ds(tr + c * tr, tr), 8, c)
                for c in range(lt):
                    for r in range(c + 1, lt):
                        nxt[own_tile(c), pl.ds(tr + r * tr, tr)] = nxt[own_tile(r), pl.ds(tr + c * tr, tr)].T
                if s < 0:
                    group_edges(t, lambda copy: copy.start())

                    @pl.when(has_ahead)
                    def _():
                        edge_ahead_copy(tile(tile_corner), 4, 0).start()

        def column_seeds(u):
            @pl.when(has_next)
            def _():
                seed_arrived(lead(u, s), inner, 1, u)
                if lt > 1:
                    seed_arrived(rest(u, s), inner, 0, u)
                group_edges(u, lambda copy: copy.start())

        def seeds_here(place, kind, u):
            if s > 0:
                @pl.when(has_next)
                def _():
                    seed_arrived(place, inner, kind, u)
                    seed_arrived(place, halo_ahead, kind + 4, u)

                @pl.when(has_next & has_behind)
                def _():
                    seed_arrived(place, halo_behind, kind + 2, u)
            else:
                @pl.when(has_next)
                def _():
                    edge_behind_copy(place, kind, u).wait_recv()

                @pl.when(has_next & has_behind)
                def _():
                    edge_ahead_copy(place, kind, u).wait_recv()

        def seeds_lead(u):
            seeds_here(lead(u, s), 1, u)

        def seeds_rest(u):
            if lt > 1:
                seeds_here(rest(u, s), 0, u)

        def near_odd():
            @pl.when(has_next & has_behind)
            def _():
                seed_arrived(tile(tile_behind), inner, 6, 0)
                if s > 0:
                    seed_arrived(tile(tile_behind), halo_behind, 7, 0)
                else:
                    edge_ahead_copy(tile(tile_behind), 4, 0).wait_recv()

            @pl.when(has_behind)
            def _():
                for i in range(lt):
                    nxt[own_tile(i), halo_behind] = nxt[tile(tile_behind), pl.ds(tr + i * tr, tr)].T
            mirror_ahead(nxt)
            near_rows(nxt, 1)

        def odd_rows(u):
            @pl.when(u != t)
            def _():
                arrive(1, u)
            left_rows(1, u, odd, inner, False)

            @pl.when(has_behind)
            def _():
                halo_behind_copy(u).start()

            @pl.when(has_ahead & (u == t))
            def _():
                halo_corner_copy(tile_corner).start()

            @pl.when(u != t)
            def _():
                halo_ahead_copy(u).start()

        def near_first():
            @pl.when(has_behind)
            def _():
                halo_corner_copy(tile_behind).wait_recv()
                halo_ahead_copy(t).wait_recv()
                for i in range(lt):
                    odd[tile(tile_behind), pl.ds(tr + i * tr, tr)] = odd[own_tile(i), halo_behind].T
            mirror_ahead(odd)
            near_rows(odd, 0)

        def first_step(u):
            halo_behind_copy(u).wait_recv()

            @pl.when(has_behind)
            def _():
                halo_ahead_copy(u).wait_recv()

            @pl.when(u == ahead)
            def _():
                near_first()
            group_rows(odd, 0, u)

            @pl.when(u != ahead)
            def _():
                arrive(0, u - s)
                left_rows(0, u - s, out_ref, everything, True)
                result_copy(u - s).start()

        def odd_step(u):
            seeds_lead(u)

            @pl.when(u == ahead)
            def _():
                near_odd()
            some_rows(nxt, 1, pl.multiple_of(lead(u, s).start, tr), tr)
            odd_rows(u - s)
            seeds_rest(u)
            if lt > 1:
                some_rows(nxt, 1, pl.multiple_of(rest(u, s).start, tr), width - tr)

        locals_in.wait()
        if s > 0:
            pass_on(1)

            @pl.when(has_behind)
            def _():
                w_start(0, t)
            near_seeds()
            groups(t, 1, has_ahead, odd_step)
        else:
            @pl.when(has_behind & has_ahead)
            def _():
                pass_one(1, ahead)
            near_seeds()

            @pl.when(has_behind)
            def _():
                w_start(0, t)

            def seed_step(u):
                @pl.when(has_behind & (u != ahead))
                def _():
                    pass_one(1, u)
                column_seeds(u)

                @pl.when(jnp.logical_not(has_behind))
                def _():
                    odd_step(u)
            groups(t, 1, has_ahead, seed_step)

            def odd_later(u):
                @pl.when((u != far_end) | (count != ranks - 2))
                def _():
                    pass_one(0, u)
            groups(t, 1, has_behind & has_ahead, odd_later)
            groups(t, 1, has_behind & has_ahead, odd_step)

        @pl.when(jnp.logical_not(has_ahead))
        def _():
            near_odd()
        odd_rows(far_end)
        diagonal(1, odd, tr)
        if s > 0:
            pass_on(0)
        else:
            @pl.when(has_ahead & (count == ranks - 2))
            def _():
                pass_one(0, far_end)
            all_edges(lambda copy: copy.wait_send())
        groups(t, 1, has_ahead, first_step)

        @pl.when(has_ahead)
        def _():
            @pl.when(jnp.logical_not(has_behind))
            def _():
                signal_partner()
            arrive(0, far_end)
            left_rows(0, far_end, out_ref, everything, True)
            wait_partner()
            result_copy(far_end).start()

        @pl.when(jnp.logical_not(has_ahead))
        def _():
            near_first()
        left_rows(0, t, out_ref, everything, False)
        diagonal(0, out_ref, 0)

        @pl.when(has_behind)
        def _():
            @pl.loop(1, ranks - count)
            def _(k):
                result_arrived(t - s * k)

        for j in (1, 0):
            groups(t, 0, has_behind, lambda u, j=j: w_copy(j, u, lambda copy: copy.wait_send()))
        seeds(lambda copy: copy.wait_send())
        groups(t, 0, has_behind, lambda u: halo_behind_copy(u).wait_send())

        @pl.when(has_ahead)
        def _():
            halo_corner_copy(tile_corner).wait_send()
        groups(t, 1, has_ahead, lambda u: halo_ahead_copy(u).wait_send())
        groups(t, 1, True, lambda u: result_copy(u).wait_send())

    for remainder, s in ((0, 1), (1, -1)):
        @pl.when(lax.rem(p, 2) == remainder)
        def _(s=s):
            triangle(s)


def per_device(parts, ranks, local_inv, seed_inv, band, pattern):
    rows, width = seed_inv.shape[1:]
    lt, tr = band.shape[1], band.shape[3]
    tiles = rows // tr
    g = 2 if lt % 2 == 0 else 1
    span = (g + 2) * tr
    dma = pltpu.SemaphoreType.DMA
    out, var = pl.pallas_call(
        functools.partial(kernel, parts, ranks),
        out_shape=(pltpu.VMEM((rows, width), F32), pltpu.VMEM((2, width), F32)),
        in_specs=[pl.BlockSpec(memory_space=pltpu.HBM)] * 3 + [pl.BlockSpec(memory_space=pltpu.SMEM)],
        out_specs=(pl.BlockSpec(memory_space=pltpu.VMEM), pl.BlockSpec(memory_space=pltpu.VMEM)),
        scratch_shapes=[
            pltpu.VMEM((rows, width + 2 * tr), F32),
            pltpu.VMEM((rows, width + 2 * tr), F32),
            pltpu.VMEM((2, tiles * 3, tr, tr), F32),
            pltpu.VMEM((2, rows + 2 * tr, width), BF16),
            pltpu.VMEM((2, rows + 2 * tr, width), BF16),
            pltpu.VMEM((2, rows, width), BF16),
            pltpu.VMEM((2, lt // g, span, g * tr), BF16),
            pltpu.VMEM((2, lt // g, span, g * tr), BF16),
            pltpu.VMEM((g * tr, span), BF16),
            pltpu.VMEM((g * tr, span), BF16),
            dma((2, ranks)),
            dma((2, ranks)),
            dma((9, max(ranks, lt))),
            dma((9, max(ranks, lt))),
            dma((5, ranks)),
            dma((5, ranks)),
            dma((3, ranks)),
            dma((3, ranks)),
            dma((ranks,)),
            dma((ranks,)),
            dma((3,)),
            pltpu.SemaphoreType.REGULAR,
        ],
        compiler_params=pltpu.CompilerParams(
            collective_id=0, has_side_effects=True, vmem_limit_bytes=58 * 1024 * 1024
        ),
    )(local_inv, seed_inv, band.reshape(2, lt * 3, tr, tr), pattern.transpose(2, 0, 1))
    return out[None], var


def solution(mesh):
    placed = (
        P("tm", None, "tile"),
        P("tm", None, "tile"),
        P("tm", "tile", None, None, None),
        P("tm", "tile", None),
    )
    return jax.shard_map(
        functools.partial(per_device, mesh.shape["tm"], mesh.shape["tile"]),
        mesh=mesh,
        in_specs=placed,
        out_specs=(P("tm", None, "tile"), P("tm", "tile")),
        check_vma=False,
    )
```

```python
import functools

import jax
import jax.numpy as jnp
from jax import lax
from jax.experimental import pallas as pl
from jax.experimental.pallas import tpu as pltpu
from jax.sharding import PartitionSpec as P

F32 = jnp.float32
BF16 = jnp.bfloat16
MESH = pl.DeviceIdType.MESH


def split(value):
    high = value.astype(BF16)
    return high, (value - high.astype(F32)).astype(BF16)


def dot(a, b):
    return lax.dot_general(a, b, (((1,), (0,)), ((), ())), preferred_element_type=F32)


def split_dot(a_high, a_low, b_high, b_low):
    return dot(a_high, b_high) + (dot(a_high, b_low) + dot(a_low, b_high))


def kernel(parts, ranks, local_ref, seed_ref, band_ref, pattern_ref, out_ref, var_ref,
           nxt, odd, wbuf, m_high, m_low, loc, wc_high, wc_low, wt_high, wt_low,
           wsend, wrecv, nsend, nrecv, esend, hsend, hrecv, rsend, rrecv, lsem, go):
    p, t = lax.axis_index("tm"), lax.axis_index("tile")
    rows, width = seed_ref.shape[1], seed_ref.shape[2]
    tr = wbuf.shape[3]
    lt = width // tr
    g = 2 if lt % 2 == 0 else 1
    span = (g + 2) * tr
    chunk = 256 if width % 256 == 0 else tr
    inner = pl.ds(tr, width)
    everything = pl.ds(0, width)
    has_next = p < parts - 1

    barrier = pltpu.get_barrier_semaphore()

    paired = parts % 2 == 0
    partner = p + 1 - 2 * lax.rem(p, 2)

    def greet(q, u):
        pl.semaphore_signal(barrier, inc=1, device_id={"tm": q, "tile": u}, device_id_type=MESH)

    @pl.loop(0, ranks)
    def _(u):
        @pl.when(u != t)
        def _():
            greet(p, u)
        if paired:
            greet(partner, u)

    reach = (0,) if paired else (-1, 0, 1)
    for a in (-1, 1):
        for b in reach:
            meet = (p + a >= 0) & (p + a < parts) & (t + b >= 0) & (t + b < ranks)

            @pl.when(meet & (p + a != partner) if paired else meet)
            def _(a=a, b=b):
                greet(p + a, t + b)
    near_tm = jnp.where(p > 0, 1, 0) + jnp.where(p < parts - 1, 1, 0) - (1 if paired else 0)
    near_tile = 1 if paired else 1 + jnp.where(t > 0, 1, 0) + jnp.where(t < ranks - 1, 1, 0)
    meets = ranks - 1 + (ranks if paired else 0) + near_tm * near_tile
    own_local = [pltpu.make_async_copy(band_ref.at[j], wbuf.at[j, pl.ds(t * lt * 3, lt * 3)], lsem.at[j]) for j in (0, 1)]
    locals_in = pltpu.make_async_copy(local_ref, loc, lsem.at[2])
    for copy in own_local[::-1]:
        copy.start()
    locals_in.start()

    @pl.when(p == parts - 1)
    def _():
        nxt[...] = jnp.zeros_like(nxt)

    for ref in (m_high, m_low):
        for j in (0, 1):
            ref[j, pl.ds(0, tr), :] = jnp.zeros((tr, width), BF16)
            ref[j, pl.ds(tr + rows, tr), :] = jnp.zeros((tr, width), BF16)
    for ref in (wc_high, wc_low, wt_high, wt_low):
        ref[...] = jnp.zeros_like(ref)
    for j in (0, 1):
        @pl.when(t > 0)
        def _(j=j):
            wbuf[j, 0] = jnp.zeros((tr, tr), F32)

        @pl.when(t < ranks - 1)
        def _(j=j):
            wbuf[j, wbuf.shape[1] - 1] = jnp.zeros((tr, tr), F32)
    for j in (1, 0):
        own_local[j].wait()
        for b in range(lt):
            for k in range(3):
                at = (j, (t * lt + b) * 3 + k)
                wbuf[at] = wbuf[at] * pattern_ref[k, j, b].astype(F32)
    pl.semaphore_wait(barrier, meets)

    def block(u):
        return pl.ds(pl.multiple_of(u * width, width), width)

    def tile(b):
        return pl.ds(pl.multiple_of(b * tr, tr), tr)

    def triangle(s):
        behind, ahead = t - s, t + s
        count = ranks - 1 - t if s > 0 else t
        has_behind, has_ahead = (t > 0, t < ranks - 1) if s > 0 else (t < ranks - 1, t > 0)
        first, last = pl.ds(tr, tr), pl.ds(width, tr)
        left, right = pl.ds(0, tr), pl.ds(tr + width, tr)
        edge_behind, edge_ahead = (first, last) if s > 0 else (last, first)
        halo_behind, halo_ahead = (left, right) if s > 0 else (right, left)
        tile_behind, tile_ahead = (t * lt - 1, (t + 1) * lt) if s > 0 else ((t + 1) * lt, t * lt - 1)
        end = ranks - 1 if s > 0 else 0
        tile_corner = (t + 1) * lt - 1 if s > 0 else t * lt

        def groups(base, start, does, action):
            number = ranks - 1 - base if s > 0 else base

            @pl.when(does)
            def _():
                @pl.loop(start, number + 1)
                def _(k):
                    action(base + s * k)


        def w_copy(j, u, action):
            for condition, skip in ((u == end, 1), (u != end, 0)):
                @pl.when(condition)
                def _(skip=skip):
                    part = wbuf.at[j, pl.ds(u * lt * 3 + (skip if s < 0 else 0), lt * 3 - skip)]
                    action(pltpu.make_async_remote_copy(
                        src_ref=part, dst_ref=part, send_sem=wsend.at[j, u], recv_sem=wrecv.at[j, u],
                        device_id={"tile": behind}, device_id_type=MESH))

        def w_start(j, u):
            w_copy(j, u, lambda copy: copy.start())

        def w_here(j, u):
            w_copy(j, u, lambda copy: copy.wait_recv())

        def pass_one(j, u):
            w_here(j, u)
            w_start(j, u)

        def pass_on(j):
            groups(t, 1, has_behind, lambda u: pass_one(j, u))

        def arrive(j, u):
            @pl.when(jnp.logical_not(has_behind))
            def _():
                w_here(j, u)


        def seed_copy(src, dst, kind, u, target):
            return pltpu.make_async_remote_copy(
                src_ref=seed_ref.at[(0,) + src], dst_ref=nxt.at[dst],
                send_sem=nsend.at[kind, u], recv_sem=nrecv.at[kind, u],
                device_id={"tm": p - 1, "tile": target}, device_id_type=MESH)

        def own_strip(c):
            return pl.ds(pl.multiple_of(t * width + c * tr, tr), width - c * tr)

        def lead(u, direction):
            return tile(u * lt if direction > 0 else (u + 1) * lt - 1)

        def rest(u, direction):
            return pl.ds(pl.multiple_of(u * width + (tr if direction > 0 else 0), tr), width - tr)

        def seeds(action):
            low, high = pl.ds(0, tr), pl.ds(width - tr, tr)
            toward, back = (low, high) if s > 0 else (high, low)
            number = t if s > 0 else ranks - 1 - t

            def pieces(u, source, place, kind, target):
                action(seed_copy((lead(u, -s), source), (lead(u, -s), place), kind + 1, u, target))
                if lt > 1:
                    action(seed_copy((rest(u, -s), source), (rest(u, -s), place), kind, u, target))

            @pl.when(p > 0)
            def _():
                @pl.when(has_ahead)
                def _():
                    row = tile(tile_ahead)
                    action(seed_copy((row, everything), (row, inner), 0, t, t))

                if s < 0:
                    @pl.when(has_behind)
                    def _():
                        corner = tile((t + 1) * lt - 1)
                        action(seed_copy((corner, toward), (corner, halo_ahead), 2, behind, behind))
                for c in range(lt):
                    strip = own_strip(c)
                    action(seed_copy((strip, pl.ds(c * tr, tr)), (strip, pl.ds(tr + c * tr, tr)), 6, c, t))

                if s < 0:
                    @pl.when(has_ahead)
                    def _():
                        pieces(t, back, halo_behind, 4, ahead)

                @pl.loop(1, number + 1)
                def _(k):
                    u = t - s * k
                    pieces(u, everything, inner, 0, t)
                    if s < 0:
                        @pl.when(has_ahead)
                        def _():
                            pieces(u, back, halo_behind, 4, ahead)

                        @pl.when(k > 1)
                        def _():
                            pieces(u, toward, halo_ahead, 2, behind)

        def seed_arrived(place, lanes, kind, u):
            pltpu.make_async_remote_copy(
                src_ref=nxt.at[place, lanes], dst_ref=nxt.at[place, lanes],
                send_sem=nsend.at[kind, u], recv_sem=nrecv.at[kind, u],
                device_id={"tile": behind}, device_id_type=MESH).wait_recv()

        def edge_copy(place, source, target_place, sent, landed, u, target):
            return pltpu.make_async_remote_copy(
                src_ref=nxt.at[place, source], dst_ref=nxt.at[place, target_place],
                send_sem=esend.at[sent], recv_sem=nrecv.at[landed, u],
                device_id={"tile": target}, device_id_type=MESH)

        def edge_ahead_copy(place, kind, u):
            return edge_copy(place, edge_ahead, halo_behind, (kind, u), kind + 2, u, ahead)

        def edge_behind_copy(place, kind, u):
            return edge_copy(place, edge_behind, halo_ahead, (kind + 2, u), kind + 4, u, behind)

        def edge_corner_copy(b, target):
            return edge_copy(tile(b), edge_ahead, halo_behind, (0, t), 2, target, ahead)

        def edges(place, kind, u, action):
            @pl.when(has_behind)
            def _():
                action(edge_behind_copy(place, kind, u))

            @pl.when((u != t) & (u != ahead))
            def _():
                action(edge_ahead_copy(place, kind, u))

        def all_edges(action):
            @pl.when(has_next)
            def _():
                @pl.loop(0, count + 1)
                def _(k):
                    group_edges(t + s * k, action)

                @pl.when(has_ahead)
                def _():
                    action(edge_corner_copy(tile_corner, ahead))

        def group_edges(u, action):
            edges(lead(u, s), 1, u, action)
            if lt > 1:
                edges(rest(u, s), 0, u, action)

        def halo_copy(place, source, target_place, kind, u, target):
            return pltpu.make_async_remote_copy(
                src_ref=odd.at[place, source], dst_ref=odd.at[place, target_place],
                send_sem=hsend.at[kind, u], recv_sem=hrecv.at[kind, u],
                device_id={"tile": target}, device_id_type=MESH)

        def halo_ahead_copy(u):
            return halo_copy(block(u), edge_ahead, halo_behind, 0, u, ahead)

        def halo_corner_copy(b, source):
            return halo_copy(tile(b), edge_ahead, halo_behind, 0, source, ahead)

        def halo_behind_copy(u):
            return halo_copy(block(u), edge_behind, halo_ahead, 1, u, behind)

        def result_copy(u):
            return pltpu.make_async_remote_copy(
                src_ref=nxt.at[block(u), inner], dst_ref=out_ref.at[block(t), everything],
                send_sem=rsend.at[u], recv_sem=rrecv.at[t],
                device_id={"tile": u}, device_id_type=MESH)

        def result_arrived(u):
            pltpu.make_async_remote_copy(
                src_ref=nxt.at[block(u), inner], dst_ref=out_ref.at[block(u), everything],
                send_sem=rsend.at[u], recv_sem=rrecv.at[u],
                device_id={"tile": behind}, device_id_type=MESH).wait_recv()

        def signal_partner():
            if paired:
                @pl.loop(0, ranks)
                def _(u):
                    @pl.when(u != t)
                    def _():
                        pl.semaphore_signal(go, inc=1, device_id={"tm": partner, "tile": u}, device_id_type=MESH)

        def wait_partner():
            if paired:
                pl.semaphore_wait(go, 1)

        def clear_halo(field, does):
            for missing, place in ((has_behind, halo_behind), (has_ahead, halo_ahead)):
                @pl.when(jnp.logical_not(missing) & does)
                def _(place=place):
                    field[:, place] = jnp.zeros((rows, tr), F32)

        def own_tile(i):
            return tile(t * lt + i)

        def mirror_ahead(field):
            @pl.when(has_ahead)
            def _():
                for i in range(lt):
                    field[own_tile(i), halo_ahead] = field[tile(tile_ahead), pl.ds(tr + i * tr, tr)].T

            @pl.when(has_ahead & has_behind)
            def _():
                field[tile(tile_behind), halo_ahead] = field[tile(tile_ahead), halo_behind].T

        def own_columns(j):
            for i in range(lt // g):
                for c in range(g):
                    for k in range(3):
                        high, low = split(wbuf[j, (t * lt + i * g + c) * 3 + k])
                        at = (j, i, pl.ds((c + k) * tr, tr), pl.ds(c * tr, tr))
                        wc_high[at] = high
                        wc_low[at] = low

        def some_rows(field, j, start, size):
            for i in range(lt // g):
                high, low = split(field[pl.ds(start, size), pl.ds(i * g * tr, span)])
                value = split_dot(high, low, wc_high[j, i], wc_low[j, i])
                at = (j, pl.ds(pl.multiple_of(start + tr, tr), size), pl.ds(i * g * tr, g * tr))
                high, low = split(value)
                m_high[at] = high
                m_low[at] = low

        def group_rows(field, j, u):
            @pl.loop(0, width // chunk)
            def _(r):
                some_rows(field, j, pl.multiple_of(u * width + r * chunk, chunk), chunk)

        def near_rows(field, j):
            @pl.when(has_behind)
            def _():
                some_rows(field, j, pl.multiple_of(tile_behind * tr, tr), tr)
            group_rows(field, j, t)

        def left_rows(j, owner, target, columns, turned):
            @pl.loop(0, lt // g)
            def _(i):
                begin = owner * lt + i * g
                for c in range(g):
                    for k in range(3):
                        high, low = split(wbuf[j, (begin + c) * 3 + k].T)
                        at = (pl.ds(c * tr, tr), pl.ds((c + k) * tr, tr))
                        wt_high[at] = high
                        wt_low[at] = low
                start = pl.multiple_of(begin * tr, tr)
                source = pl.ds(start, span)
                value = split_dot(wt_high[...], wt_low[...], m_high[j, source, :], m_low[j, source, :])
                place = pl.ds(start, g * tr)
                value = loc[j, place, :].astype(F32) + value
                target[place, columns] = value
                if turned:
                    for c in range(g):
                        lanes = pl.ds(pl.multiple_of(tr + (i * g + c) * tr, tr), tr)
                        for q in range(lt):
                            nxt[tile(owner * lt + q), lanes] = value[c * tr:(c + 1) * tr, q * tr:(q + 1) * tr].T

        def diagonal(index, field, offset):
            eye = lax.broadcasted_iota(jnp.int32, (tr, tr), 0) == lax.broadcasted_iota(jnp.int32, (tr, tr), 1)
            for c in range(lt):
                part = field[own_tile(c), pl.ds(offset + c * tr, tr)]
                var_ref[pl.ds(index, 1), pl.ds(c * tr, tr)] = jnp.sum(jnp.where(eye, part, 0.0), axis=0, keepdims=True)

        far_end = t + s * count

        @pl.when(has_behind)
        def _():
            w_start(1, t)
        seeds(lambda copy: copy.start())
        clear_halo(odd, True)
        clear_halo(nxt, has_next)
        own_columns(1)
        own_columns(0)

        def near_seeds():
            @pl.when(has_next)
            def _():
                for c in range(lt):
                    seed_arrived(own_strip(c), pl.ds(tr + c * tr, tr), 6, c)
                for c in range(lt):
                    for r in range(c + 1, lt):
                        nxt[own_tile(c), pl.ds(tr + r * tr, tr)] = nxt[own_tile(r), pl.ds(tr + c * tr, tr)].T
                if s < 0:
                    group_edges(t, lambda copy: copy.start())

                    @pl.when(has_ahead)
                    def _():
                        edge_corner_copy(tile_corner, ahead).start()

        def column_seeds(u):
            @pl.when(has_next)
            def _():
                seed_arrived(lead(u, s), inner, 1, u)
                if lt > 1:
                    seed_arrived(rest(u, s), inner, 0, u)
                group_edges(u, lambda copy: copy.start())

        def seeds_here(place, kind, u):
            if s > 0:
                @pl.when(has_next)
                def _():
                    seed_arrived(place, inner, kind, u)
                    seed_arrived(place, halo_ahead, kind + 4, u)

                @pl.when(has_next & has_behind)
                def _():
                    seed_arrived(place, halo_behind, kind + 2, u)
            else:
                @pl.when(has_next)
                def _():
                    edge_behind_copy(place, kind, u).wait_recv()

                @pl.when(has_next & has_behind)
                def _():
                    edge_ahead_copy(place, kind, u).wait_recv()

        def seeds_lead(u):
            seeds_here(lead(u, s), 1, u)

        def seeds_rest(u):
            if lt > 1:
                seeds_here(rest(u, s), 0, u)

        def near_odd():
            @pl.when(has_next & has_behind)
            def _():
                seed_arrived(tile(tile_behind), inner, 0, t)
                if s > 0:
                    seed_arrived(tile(tile_behind), halo_behind, 2, t)
                else:
                    edge_corner_copy(tile_behind, t).wait_recv()

            @pl.when(has_behind)
            def _():
                for i in range(lt):
                    nxt[own_tile(i), halo_behind] = nxt[tile(tile_behind), pl.ds(tr + i * tr, tr)].T
            mirror_ahead(nxt)
            near_rows(nxt, 1)

        def odd_rows(u):
            @pl.when(u != t)
            def _():
                arrive(1, u)
            left_rows(1, u, odd, inner, False)

            @pl.when(has_behind)
            def _():
                halo_behind_copy(u).start()

            @pl.when(has_ahead & (u == t))
            def _():
                halo_corner_copy(tile_corner, t).start()

            @pl.when(u != t)
            def _():
                halo_ahead_copy(u).start()

        def near_first():
            @pl.when(has_behind)
            def _():
                halo_corner_copy(tile_behind, behind).wait_recv()
                halo_ahead_copy(t).wait_recv()
                for i in range(lt):
                    odd[tile(tile_behind), pl.ds(tr + i * tr, tr)] = odd[own_tile(i), halo_behind].T
            mirror_ahead(odd)
            near_rows(odd, 0)

        def first_step(u):
            halo_behind_copy(u).wait_recv()

            @pl.when(has_behind)
            def _():
                halo_ahead_copy(u).wait_recv()

            @pl.when(u == ahead)
            def _():
                near_first()
            group_rows(odd, 0, u)

            @pl.when(u != ahead)
            def _():
                arrive(0, u - s)
                left_rows(0, u - s, out_ref, everything, True)
                result_copy(u - s).start()

        def odd_step(u):
            seeds_lead(u)

            @pl.when(u == ahead)
            def _():
                near_odd()
            some_rows(nxt, 1, pl.multiple_of(lead(u, s).start, tr), tr)
            odd_rows(u - s)
            seeds_rest(u)
            if lt > 1:
                some_rows(nxt, 1, pl.multiple_of(rest(u, s).start, tr), width - tr)

        locals_in.wait()
        if s > 0:
            pass_on(1)

            @pl.when(has_behind)
            def _():
                w_start(0, t)
            near_seeds()
            groups(t, 1, has_ahead, odd_step)
        else:
            @pl.when(has_behind & has_ahead)
            def _():
                pass_one(1, ahead)
            near_seeds()

            @pl.when(has_behind)
            def _():
                w_start(0, t)

            def seed_step(u):
                @pl.when(has_behind & (u != ahead))
                def _():
                    pass_one(1, u)
                column_seeds(u)

                @pl.when(jnp.logical_not(has_behind))
                def _():
                    odd_step(u)
            groups(t, 1, has_ahead, seed_step)

            def odd_later(u):
                @pl.when((u != far_end) | (count != ranks - 2))
                def _():
                    pass_one(0, u)
            groups(t, 1, has_behind & has_ahead, odd_later)
            groups(t, 1, has_behind & has_ahead, odd_step)

        @pl.when(jnp.logical_not(has_ahead))
        def _():
            near_odd()
        odd_rows(far_end)
        diagonal(1, odd, tr)
        if s > 0:
            pass_on(0)
        else:
            @pl.when(has_ahead & (count == ranks - 2))
            def _():
                pass_one(0, far_end)
            all_edges(lambda copy: copy.wait_send())
        groups(t, 1, has_ahead, first_step)

        @pl.when(has_ahead)
        def _():
            @pl.when(jnp.logical_not(has_behind))
            def _():
                signal_partner()
            arrive(0, far_end)
            left_rows(0, far_end, out_ref, everything, True)
            wait_partner()
            result_copy(far_end).start()

        @pl.when(jnp.logical_not(has_ahead))
        def _():
            near_first()
        left_rows(0, t, out_ref, everything, False)
        diagonal(0, out_ref, 0)

        for j in (1, 0):
            groups(t, 0, has_behind, lambda u, j=j: w_copy(j, u, lambda copy: copy.wait_send()))
        seeds(lambda copy: copy.wait_send())
        groups(t, 0, has_behind, lambda u: halo_behind_copy(u).wait_send())

        @pl.when(has_ahead)
        def _():
            halo_corner_copy(tile_corner, t).wait_send()
        groups(t, 1, has_ahead, lambda u: halo_ahead_copy(u).wait_send())
        groups(t, 1, True, lambda u: result_copy(u).wait_send())

        @pl.when(has_behind)
        def _():
            @pl.loop(1, ranks - count)
            def _(k):
                result_arrived(t - s * k)

    for remainder, s in ((0, 1), (1, -1)):
        @pl.when(lax.rem(p, 2) == remainder)
        def _(s=s):
            triangle(s)


def per_device(parts, ranks, local_inv, seed_inv, band, pattern):
    rows, width = seed_inv.shape[1:]
    lt, tr = band.shape[1], band.shape[3]
    tiles = rows // tr
    g = 2 if lt % 2 == 0 else 1
    span = (g + 2) * tr
    dma = pltpu.SemaphoreType.DMA
    out, var = pl.pallas_call(
        functools.partial(kernel, parts, ranks),
        out_shape=(pltpu.VMEM((rows, width), F32), pltpu.VMEM((2, width), F32)),
        in_specs=[pl.BlockSpec(memory_space=pltpu.HBM)] * 3 + [pl.BlockSpec(memory_space=pltpu.SMEM)],
        out_specs=(pl.BlockSpec(memory_space=pltpu.VMEM), pl.BlockSpec(memory_space=pltpu.VMEM)),
        scratch_shapes=[
            pltpu.VMEM((rows, width + 2 * tr), F32),
            pltpu.VMEM((rows, width + 2 * tr), F32),
            pltpu.VMEM((2, tiles * 3, tr, tr), F32),
            pltpu.VMEM((2, rows + 2 * tr, width), BF16),
            pltpu.VMEM((2, rows + 2 * tr, width), BF16),
            pltpu.VMEM((2, rows, width), BF16),
            pltpu.VMEM((2, lt // g, span, g * tr), BF16),
            pltpu.VMEM((2, lt // g, span, g * tr), BF16),
            pltpu.VMEM((g * tr, span), BF16),
            pltpu.VMEM((g * tr, span), BF16),
            dma((2, ranks)),
            dma((2, ranks)),
            dma((7, max(ranks, lt))),
            dma((7, max(ranks, lt))),
            dma((4, ranks)),
            dma((2, ranks)),
            dma((2, ranks)),
            dma((ranks,)),
            dma((ranks,)),
            dma((3,)),
            pltpu.SemaphoreType.REGULAR,
        ],
        compiler_params=pltpu.CompilerParams(
            collective_id=0, has_side_effects=True, vmem_limit_bytes=58 * 1024 * 1024
        ),
    )(local_inv, seed_inv, band.reshape(2, lt * 3, tr, tr), pattern.transpose(2, 0, 1))
    return out[None], var


def solution(mesh):
    placed = (
        P("tm", None, "tile"),
        P("tm", None, "tile"),
        P("tm", "tile", None, None, None),
        P("tm", "tile", None),
    )
    return jax.shard_map(
        functools.partial(per_device, mesh.shape["tm"], mesh.shape["tile"]),
        mesh=mesh,
        in_specs=placed,
        out_specs=(P("tm", None, "tile"), P("tm", "tile")),
        check_vma=False,
    )
```
